32 devices in a mesh: row: 4 (over z), col: 8 (over y, x, core).
Axes of the slice: x: 2, y: 2, z: 4, core: 2. Of those that a mesh axis runs over, the one named last changes fastest.
Arguments:
- amplitudes: float32 [1024, 8192], P('col', 'row'), may hold values from -6 to 6
- integrals: float32 [8192, 32768], P('row', 'col'), may hold values from -0.0625 to 0.0625
- integral_mask: int32 [64, 256], P('row', 'col'), may hold values 0 or 1
- denominators: float32 [1024, 32768], P('row', 'col'), may hold values from 0.25 to 2
- cycle_tiles: float32 [32768, 512], P('col'), may hold values from -0.25 to 0.25
- cycle_mask: int32 [256, 4], P('col'), may hold values 0 or 1
- destination: int32 [1024, 256], P('row', 'col'), may hold values from 0 to 262143, as said below
Outputs:
- update: float32 [1024, 32768], P('row', 'col')
- cycle_term: float32 [1024, 32768], P('row', 'col')
The draws below stay inside these ranges and needn't reach their ends.
Inputs may be any that keep to these rules, and one draw needn't show every extreme that they name: destination is a permutation of the units. Numbering a unit (r, t) as r * 256 + t and cutting the units into blocks of 256 rows by 32 tiles, every block sends exactly 256 of its units to every block.
All inputs are finite; a program needn't handle non-finite values. No bound on the sum of `integral_mask` or of `cycle_mask` on one device may be relied on, other than what follows from the above.
Results may differ from the reference program's by a relative error of at most 0.0003.
Values sent between devices are 32-bit elements; how exact they have to be, the bound alone decides.
A program may use at most 192 MiB of HBM per device.

```python
import math
import jax
import jax.numpy as jnp
from jax import lax

V2 = 32768
TILE = 128
RB = 512
OCC = 1024
VT = 256
CD = 8192
IJ_DEV = 256
TPD = 32
CAP = 256


def draw_destination(key, part):
    base = jax.random.fold_in(key, 7)
    key_src, key_dst = jax.random.split(base)
    units = IJ_DEV * TPD
    row_blocks = OCC // IJ_DEV
    col_blocks = VT // TPD
    ndev = row_blocks * col_blocks
    src_perm = jax.vmap(lambda k: jax.random.permutation(k, units))(jax.random.split(key_src, ndev)).astype(jnp.int32)
    dst_perm = jax.vmap(lambda k: jax.random.permutation(k, units))(jax.random.split(key_dst, ndev)).astype(jnp.int32)
    dvec = jnp.arange(ndev, dtype=jnp.int32)[:, None, None]
    svec = jnp.arange(ndev, dtype=jnp.int32)[None, :, None]
    kvec = jnp.arange(CAP, dtype=jnp.int32)[None, None, :]
    slot = dst_perm[dvec, svec * CAP + kvec]
    local = src_perm[svec, dvec * CAP + kvec]

    def global_unit(device, loc):
        prow = device // col_blocks
        pcol = device % col_blocks
        return (prow * IJ_DEV + loc // TPD) * VT + pcol * TPD + loc % TPD
    out_q = global_unit(jnp.broadcast_to(dvec, slot.shape), slot)
    in_q = global_unit(jnp.broadcast_to(svec, local.shape), local)
    dest = jnp.zeros((OCC * VT,), jnp.int32).at[in_q.reshape(-1)].set(out_q.reshape(-1))
    return dest.reshape(OCC, VT)


def touch_ends(values, own_key, smallest, top_value):
    shape = values.shape
    spot = [jax.random.randint(jax.random.fold_in(own_key, axis), (), 0, shape[axis]) for axis in range(len(shape))]
    values = values.at[tuple(spot)].set(smallest)
    longest = shape.index(max(shape))
    spot[longest] = (spot[longest] + 1) % shape[longest]
    return values.at[tuple(spot)].set(top_value)


def level_of(rng, dims, cuts, low, largest):
    def one(axis_at, parts):
        draws = jax.random.uniform(jax.random.fold_in(jax.random.fold_in(rng, 6), axis_at), (parts,), jnp.float32, low / len(cuts), largest / len(cuts))
        return jnp.repeat(jnp.exp(draws), dims[axis_at] // parts).reshape((-1,) + (1,) * (len(dims) - axis_at - 1))

    loudness = one(*cuts[0])
    for cut in cuts[1:]:
        loudness = loudness * one(*cut)
    return loudness


def gaussian(rng, dims, deviation, most, cuts=(), kind=jnp.bfloat16):
    level = level_of(rng, dims, cuts, -0.22, 0.18) if cuts else 1.0
    array = jax.random.normal(rng, dims, jnp.float32) * deviation * level
    return jnp.minimum(jnp.maximum(array, -most), most).astype(kind)


def setup_inputs(seed: int = 0) -> dict:
    key_list = jax.random.split(jax.random.key(seed), 8)
    return {
        "amplitudes": gaussian(key_list[0], (OCC, CD), 1.0, 6.0, ((0, 8), (1, 4)), jnp.float32),
        "integrals": gaussian(key_list[1], (CD, V2), CD ** -0.5, 0.0625, ((0, 4), (1, 8)), jnp.float32),
        "integral_mask": touch_ends((jax.random.randint(key_list[2], (CD // TILE, VT), 0, 5) < 3).astype(jnp.int32), jax.random.fold_in(key_list[2], 1), 0, 1),
        "denominators": jnp.clip(jnp.exp(math.log(2.0) - 2.0794415 * jax.random.uniform(key_list[3], (OCC, V2), jnp.float32) ** level_of(key_list[3], (OCC, V2), ((0, 4), (1, 8)), -0.2, 0.2)), 0.25, 2.0),
        "cycle_tiles": gaussian(key_list[4], (V2, RB), RB ** -0.5, 0.25, ((0, 8),), jnp.float32),
        "cycle_mask": touch_ends((jax.random.randint(key_list[5], (VT, RB // TILE), 0, 5) < 3).astype(jnp.int32), jax.random.fold_in(key_list[5], 1), 0, 1),
        "destination": draw_destination(jax.random.fold_in(key_list[7], 71), 0),
    }


def reference(amplitudes, integrals, integral_mask, denominators, cycle_tiles, cycle_mask, destination):
    width = V2 // 16
    tiles_blk = width // TILE
    mask_f = integral_mask.astype(jnp.float32)

    def column_block(index):
        start = (index * width).astype(jnp.int32)
        block = lax.dynamic_slice_in_dim(integrals, start, width, 1)
        mblock = lax.dynamic_slice_in_dim(mask_f, (index * tiles_blk).astype(jnp.int32), tiles_blk, 1)
        masked = (block.reshape(CD // TILE, TILE, tiles_blk, TILE) * mblock[:, None, :, None]).reshape(CD, width)
        return jnp.dot(amplitudes, masked, precision=lax.Precision.HIGHEST, preferred_element_type=jnp.float32)

    blocks = lax.map(column_block, jnp.arange(16, dtype=jnp.int32))
    residual = jnp.transpose(blocks, (1, 0, 2)).reshape(OCC, V2)
    units = residual.reshape(OCC * VT, TILE)
    moved = jnp.zeros_like(units).at[destination.reshape(-1)].set(units).reshape(OCC, V2)
    update = moved / denominators
    rmask = cycle_mask.astype(jnp.float32)
    cycle = (cycle_tiles.reshape(VT, TILE, RB // TILE, TILE) * rmask[:, None, :, None]).reshape(V2 // RB, RB, RB)
    cycle_term = jnp.einsum("okr,krs->oks", update.reshape(OCC, V2 // RB, RB), cycle,
                           precision=lax.Precision.HIGHEST, preferred_element_type=jnp.float32).reshape(OCC, V2)
    return update, cycle_term
```

```python
import functools
import jax
import jax.numpy as jnp
from jax import lax
from jax.experimental import pallas as pl
from jax.experimental.pallas import tpu as pltpu
from jax.sharding import PartitionSpec as P

TILE = 128
F32 = jnp.float32
BF16 = jnp.bfloat16
CHUNKS = 4


def split(x):
    hi = x.astype(BF16)
    return hi, (x - hi.astype(F32)).astype(BF16)


def dot(a, b):
    return jnp.dot(a, b, preferred_element_type=F32)


def product_kernel(nblk, first_tile, tpb, off_ref, mask_ref, a_ref, b_ref, *rest):
    outs, (a_hi, a_lo, b_hi, b_lo) = rest[:-4], rest[-4:]
    rows, depth = a_ref.shape
    blk = rows // nblk
    step = pl.program_id(0)

    @pl.when(step == 0)
    def _():
        for j in range(nblk):
            src = pl.multiple_of(off_ref[j] * blk, blk)
            hi, lo = split(a_ref[pl.ds(src, blk), :])
            a_hi[pl.ds(j * blk, blk), :] = hi
            a_lo[pl.ds(j * blk, blk), :] = lo

    @pl.loop(0, depth // TILE)
    def _(c):
        at = pl.ds(pl.multiple_of(c * TILE, TILE), TILE)
        for t in range(tpb):
            cols = pl.ds(t * TILE, TILE)
            m = mask_ref[c, first_tile + step * tpb + t].astype(F32)
            hi, lo = split(b_ref[at, cols] * m)
            b_hi[at, cols] = hi
            b_lo[at, cols] = lo

    big = rows // 2
    piece = rows // len(outs)
    per = big // piece if big >= piece else 1
    for h in range(2):
        at = pl.ds(h * big, big)
        acc = dot(a_hi[at, :], b_hi[...]) + dot(a_lo[at, :], b_hi[...]) + dot(a_hi[at, :], b_lo[...])
        for t in range(tpb):
            col = acc[:, t * TILE:(t + 1) * TILE]
            if len(outs) == 1:
                outs[0][t, at, :] = col
            else:
                for q in range(per):
                    outs[h * per + q][t, :, :] = col[q * piece:(q + 1) * piece]


def product(amps, integrals, mask, offsets, chunk, nblk, npieces):
    rows, depth = amps.shape
    cols = integrals.shape[1]
    width = cols // CHUNKS
    tpb = min(4, width // TILE)
    bn = tpb * TILE
    steps = width // bn
    piece = rows // npieces
    out = jax.ShapeDtypeStruct((width // TILE, piece, TILE), F32)
    return pl.pallas_call(
        functools.partial(product_kernel, nblk, chunk * (width // TILE), tpb),
        out_shape=[out] * npieces,
        grid_spec=pltpu.PrefetchScalarGridSpec(
            num_scalar_prefetch=2,
            grid=(steps,),
            in_specs=[
                pl.BlockSpec((rows, depth), lambda i, o, m: (0, 0), pipeline_mode=pl.Buffered(1)),
                pl.BlockSpec((depth, bn), lambda i, o, m: (0, chunk * steps + i)),
            ],
            out_specs=[pl.BlockSpec((tpb, piece, TILE), lambda i, o, m: (i, 0, 0))] * npieces,
            scratch_shapes=[
                pltpu.VMEM((rows, depth), BF16),
                pltpu.VMEM((rows, depth), BF16),
                pltpu.VMEM((depth, bn), BF16),
                pltpu.VMEM((depth, bn), BF16),
            ],
        ),
        cost_estimate=pl.CostEstimate(
            flops=6 * rows * depth * width,
            bytes_accessed=4 * (rows * depth + depth * width + rows * width),
            transcendentals=0,
        ),
        compiler_params=pltpu.CompilerParams(vmem_limit_bytes=56 * 2**20),
        name="product",
    )(offsets, mask, amps, integrals)


def gather_kernel(idx_ref, x_ref, o_ref):
    n = o_ref.shape[0]
    base = pl.program_id(0) * n

    @pl.loop(0, n // 16)
    def _(i):
        for u in range(16):
            k = i * 16 + u
            o_ref[pl.ds(k, 1), :] = x_ref[pl.ds(idx_ref[base + k], 1), :]


def gather_units(units, idx):
    n = units.shape[0]
    bn = min(1024, n)
    return pl.pallas_call(
        gather_kernel,
        out_shape=jax.ShapeDtypeStruct(units.shape, F32),
        grid_spec=pltpu.PrefetchScalarGridSpec(
            num_scalar_prefetch=1,
            grid=(n // bn,),
            in_specs=[pl.BlockSpec(units.shape, lambda i, s: (0, 0), pipeline_mode=pl.Buffered(1))],
            out_specs=pl.BlockSpec((bn, TILE), lambda i, s: (i, 0)),
        ),
        compiler_params=pltpu.CompilerParams(vmem_limit_bytes=24 * 2**20),
        name="gather_units",
    )(idx, units)


def finish_kernel(tiles, tpb, idx_ref, mask_ref, got_ref, den_ref, cyc_ref, upd_ref, term_ref, moved, c_hi, c_lo):
    rows = den_ref.shape[0]
    k = pl.program_id(0)

    @pl.loop(0, rows // 8)
    def _(i):
        for u in range(8):
            r = i * 8 + u
            for t in range(tpb):
                q = idx_ref[r * tiles + k * tpb + t]
                moved[t, pl.ds(r, 1), :] = got_ref[pl.ds(q, 1), :]

    for u in range(tpb):
        for s in range(tpb):
            at = (pl.ds(u * TILE, TILE), pl.ds(s * TILE, TILE))
            hi, lo = split(cyc_ref[at] * mask_ref[k * tpb + u, s].astype(F32))
            c_hi[at] = hi
            c_lo[at] = lo
    upd = jnp.concatenate([moved[t] for t in range(tpb)], axis=1) / den_ref[...]
    upd_ref[...] = upd
    hi, lo = split(upd)
    term_ref[...] = dot(hi, c_hi[...]) + dot(lo, c_hi[...]) + dot(hi, c_lo[...])


def finish(got, inv, denominators, cycle_tiles, cycle_mask):
    rows, cols = denominators.shape
    rb = cycle_tiles.shape[1]
    out = jax.ShapeDtypeStruct((rows, cols), F32)
    block = pl.BlockSpec((rows, rb), lambda i, s, m: (0, i))
    return pl.pallas_call(
        functools.partial(finish_kernel, cols // TILE, rb // TILE),
        out_shape=[out, out],
        grid_spec=pltpu.PrefetchScalarGridSpec(
            num_scalar_prefetch=2,
            grid=(cols // rb,),
            in_specs=[
                pl.BlockSpec(got.shape, lambda i, s, m: (0, 0), pipeline_mode=pl.Buffered(1)),
                block,
                pl.BlockSpec((rb, rb), lambda i, s, m: (i, 0)),
            ],
            out_specs=[block, block],
            scratch_shapes=[
                pltpu.VMEM((rb // TILE, rows, TILE), F32),
                pltpu.VMEM((rb, rb), BF16),
                pltpu.VMEM((rb, rb), BF16),
            ],
        ),
        compiler_params=pltpu.CompilerParams(vmem_limit_bytes=40 * 2**20),
        name="finish",
    )(inv, cycle_mask, got, denominators, cycle_tiles)


def routes(destination, nrow, ncol):
    local_rows, local_tiles = destination.shape
    vt = local_tiles * ncol
    units = local_rows * local_tiles
    half = local_rows // 2
    tc = local_tiles // CHUNKS
    flat = destination.reshape(2, half, CHUNKS, tc).transpose(2, 0, 3, 1).reshape(-1)
    out_row = flat // vt
    out_tile = flat % vt
    owner = out_row // local_rows * ncol + out_tile // local_tiles
    place = out_row % local_rows * local_tiles + out_tile % local_tiles
    iota = lax.iota(jnp.int32, units)
    key, order = lax.sort((owner * units + place, iota), num_keys=1, is_stable=False)
    ndev = nrow * ncol
    places = (key % units).astype(F32).reshape(ndev, units // ndev)
    got_place = lax.all_to_all(places, ("row", "col"), split_axis=0, concat_axis=0, tiled=True)
    _, inv = lax.sort((got_place.reshape(-1).astype(jnp.int32), iota), num_keys=1, is_stable=False)
    return order, inv


def body(amplitudes, integrals, integral_mask, denominators, cycle_tiles, cycle_mask, destination):
    nrow = lax.axis_size("row")
    ncol = lax.axis_size("col")
    me = lax.axis_index("row")
    amps = lax.all_gather(amplitudes, "col", axis=0, tiled=True)
    order, inv = routes(destination, nrow, ncol)
    local_rows = destination.shape[0]
    half = local_rows // 2
    pieces = []
    if nrow == 4:
        up = [(i, (i + 1) % nrow) for i in range(nrow)]
        down = [(i, (i - 1) % nrow) for i in range(nrow)]
        offsets = jnp.stack([(me + d) % nrow for d in (2, 1, 3, 0)]).astype(jnp.int32)
        sent, landed = [], []
        for c in range(CHUNKS):
            if c >= 2:
                after = sent[c - 2] + (landed[c - 3] if c >= 3 else [])
                offsets = lax.optimization_barrier([offsets] + after)[0]
            far_a, far_b, up_a, up_b, dn_a, dn_b, own_a, own_b = product(
                amps, integrals, integral_mask, offsets, c, nrow, 2 * nrow)
            in_a = lax.ppermute(far_a, "row", up)
            in_b = lax.ppermute(far_b, "row", down)
            direct_b = lax.ppermute(up_b, "row", up)
            direct_a = lax.ppermute(dn_a, "row", down)
            next_a, next_b = up_a + in_a, dn_b + in_b
            sum_a = lax.ppermute(next_a, "row", up)
            sum_b = lax.ppermute(next_b, "row", down)
            sent.append([next_a, next_b, direct_a, direct_b])
            landed.append([sum_a, sum_b])
            pieces.append(own_a + direct_a + sum_a)
            pieces.append(own_b + direct_b + sum_b)
    else:
        offsets = lax.iota(jnp.int32, nrow)
        for c in range(CHUNKS):
            (part,) = product(amps, integrals, integral_mask, offsets, c, nrow, 1)
            summed = lax.psum_scatter(part, "row", scatter_dimension=1, tiled=True)
            pieces.append(summed[:, :half])
            pieces.append(summed[:, half:])
    units = jnp.concatenate([p.reshape(-1, TILE) for p in pieces], axis=0)
    sending = gather_units(units, order)
    ndev = nrow * ncol
    got = lax.all_to_all(sending.reshape(ndev, -1, TILE), ("row", "col"), split_axis=0, concat_axis=0, tiled=True)
    return tuple(finish(got.reshape(-1, TILE), inv, denominators, cycle_tiles, cycle_mask))


MESH = pl.DeviceIdType.MESH
SLICE = 512
UNROLL = 16


def exchange_kernel(nrow, ncol, mask_ref, amps, integ, keys, got, gotp, aall, oall,
                    st, ast, ah, al, bh, bl, part, group, ru, rd, idx,
                    a_s, a_r, o_s, o_r, p_s, p_r, u_s, u_r, d_s, d_r, f_s, f_r, b_sem, l_sem, credit_u, credit_d):
    z = lax.axis_index("row")
    c = lax.axis_index("col")
    last = nrow - 1
    arows, depth = amps.shape
    nblk, cap = got.shape[0], got.shape[1]
    units = nblk * cap
    nsl, _, width = bh.shape
    tps = width // TILE
    rows = ah.shape[0]
    nk = last * ncol
    core = c % 2
    cx = c // 2 % 2
    cy = c // 4

    def peer(k):
        px = (cx + k // 2 % 2) % 2
        py = (cy + k // 4) % 2
        return (py * 2 + px) * 2 + (core + k % 2) % 2

    def block_of(j):
        return (cy + j // 2) % 2 * 2 + (cx + j % 2) % 2

    def amps_copy(k):
        return pltpu.make_async_remote_copy(amps, aall.at[c], a_s.at[k], a_r.at[k], (z, peer(k)), MESH)

    def keys_copy(dz):
        return pltpu.make_async_remote_copy(
            keys, oall.at[pl.ds(z * nblk, nblk)], o_s.at[dz], o_r.at[dz], ((z + dz) % nrow, c), MESH)

    def up_copy(k):
        g = (last - k // ncol) * ncol + k % ncol
        return pltpu.make_async_remote_copy(group.at[g], ru.at[k], u_s.at[k], u_r.at[k], ((z + 1) % nrow, c), MESH)

    def down_copy(k):
        return pltpu.make_async_remote_copy(
            group.at[k], rd.at[k], d_s.at[k], d_r.at[k], ((z + nrow - 1) % nrow, c), MESH)

    def final_copy(j, cc):
        s = block_of(j) * ncol + c
        return pltpu.make_async_remote_copy(group.at[z * ncol + cc], got.at[s], f_s.at[cc], f_r.at[s], (z, cc), MESH)

    def final_local(j):
        return pltpu.make_async_copy(group.at[z * ncol + c], got.at[block_of(j) * ncol + c], f_s.at[c])

    def load_cols(s, slot):
        at = pl.ds(pl.multiple_of(s * width, width), width)
        return pltpu.make_async_copy(integ.at[:, at], st.at[slot], b_sem.at[slot])

    def load_amps(j):
        r = block_of(j)
        for i in range(2):
            e = (i + core) % 2
            dst, sem = ast.at[i], l_sem.at[i]
            own = (j + e) == 0

            @pl.when(own)
            def _():
                pltpu.make_async_copy(amps, dst, sem).start()

            @pl.when(jnp.logical_not(own))
            def _():
                amps_copy(j * 2 + e).wait_recv()
                pltpu.make_async_copy(aall.at[r * 2 + i], dst, sem).start()

        for i in range(2):
            pltpu.make_async_copy(amps, ast.at[i], l_sem.at[i]).wait()

            @pl.loop(0, arows // 16)
            def _(n):
                at = pl.ds(pl.multiple_of(n * 16, 16), 16)
                to = pl.ds(pl.multiple_of(i * arows + n * 16, 16), 16)
                hi, lo = split(ast[i, at, :])
                ah[to, :] = hi
                al[to, :] = lo

    def dots(s):
        acc = dot(ah[...], bh[s]) + dot(al[...], bh[s]) + dot(ah[...], bl[s])
        for t in range(tps):
            at = pl.ds(pl.multiple_of((s * tps + t) * rows, rows), rows)
            part[at, :] = acc[:, t * TILE:(t + 1) * TILE]

    def split_cols(s, slot):
        @pl.loop(0, depth // TILE)
        def _(n):
            at = pl.ds(pl.multiple_of(n * TILE, TILE), TILE)
            for t in range(tps):
                cols = pl.ds(t * TILE, TILE)
                hi, lo = split(st[slot, at, cols] * mask_ref[n, s * tps + t].astype(F32))
                bh[s, at, cols] = hi
                bl[s, at, cols] = lo

    for slot in range(2):
        load_cols(slot, slot).start()
    barrier = pltpu.get_barrier_semaphore()
    for k in range(1, ncol):
        pl.semaphore_signal(barrier, 1, device_id=(z, peer(k)), device_id_type=MESH)
    for dz in range(1, nrow):
        pl.semaphore_signal(barrier, 1, device_id=((z + dz) % nrow, c), device_id_type=MESH)
    pl.semaphore_wait(barrier, ncol - 1 + nrow - 1)

    for dz in range(1, nrow):
        keys_copy(dz).start()
    for k in range(1, ncol):
        amps_copy(k).start()
    own_keys = pltpu.make_async_copy(keys, oall.at[pl.ds(z * nblk, nblk)], l_sem.at[2])
    own_keys.start()

    load_amps(0)

    @pl.loop(0, nsl)
    def _(s):
        slot = s % 2
        load_cols(s, slot).wait()
        split_cols(s, slot)

        @pl.when(s < nsl - 2)
        def _():
            load_cols(s + 2, slot).start()

        dots(s)

    own_keys.wait()
    for dz in range(1, nrow):
        keys_copy(dz).wait()
    to_scalar = pltpu.make_async_copy(oall, idx, l_sem.at[2])
    to_scalar.start()

    def places_remote(r, cc):
        return pltpu.make_async_remote_copy(
            oall.at[r * nblk + z * ncol + cc], gotp.at[r * ncol + c], p_s.at[r * ncol + cc], p_r.at[r * ncol + c],
            (z, cc), MESH)

    def places_local(r):
        return pltpu.make_async_copy(oall.at[r * nblk + z * ncol + c], gotp.at[r * ncol + c], p_s.at[r * ncol + c])

    @pl.loop(0, nblk)
    def _(n):
        r = n // ncol
        cc = n % ncol

        @pl.when(cc == c)
        def _():
            places_local(r).start()

        @pl.when(cc != c)
        def _():
            places_remote(r, cc).start()

    to_scalar.wait()

    def step(j, k):
        d = last - k // ncol
        cc = k % ncol
        more = j < nrow - 1

        @pl.when(jnp.logical_and(z >= 1, d >= z))
        def _():
            g = d * ncol + cc
            up_copy(k).wait_recv()
            group[g] += ru[k]

            @pl.when(more)
            def _():
                pl.semaphore_signal(credit_u, 1, device_id=((z + nrow - 1) % nrow, c), device_id_type=MESH)

            @pl.when(d > z)
            def _():
                @pl.when(j > 0)
                def _():
                    pl.semaphore_wait(credit_u, 1)

                up_copy(k).start()

        e = k // ncol

        @pl.when(jnp.logical_and(z < last, e <= z))
        def _():
            down_copy(k).wait_recv()
            group[k] += rd[k]

            @pl.when(more)
            def _():
                pl.semaphore_signal(credit_d, 1, device_id=((z + 1) % nrow, c), device_id_type=MESH)

            @pl.when(e < z)
            def _():
                @pl.when(j > 0)
                def _():
                    pl.semaphore_wait(credit_d, 1)

                down_copy(k).start()

        @pl.when(e == z * (last - z))
        def _():
            @pl.when(cc == c)
            def _():
                final_local(j).start()

            @pl.when(cc != c)
            def _():
                final_copy(j, cc).start()

    def wait_sent(g):
        d = g // ncol
        cc = g % ncol

        @pl.when(d > z)
        def _():
            up_copy((last - d) * ncol + cc).wait_send()

        @pl.when(d < z)
        def _():
            down_copy(g).wait_send()

        @pl.when(jnp.logical_and(d == z, cc == c))
        def _():
            final_local(0).wait()

        @pl.when(jnp.logical_and(d == z, cc != c))
        def _():
            final_copy(0, cc).wait_send()

    low = 1 - z // 2
    lag = 2
    per = nk // (nsl - lag)

    @pl.loop(0, nrow)
    def _(j):
        base = block_of(j) * nblk

        @pl.loop(0, nblk)
        def _(n):
            q = n // ncol
            cc = n % ncol
            d = low * (last - q) + (1 - low) * q
            g = d * ncol + cc

            @pl.when(j > 0)
            def _():
                wait_sent(g)

            @pl.loop(0, cap // UNROLL)
            def _(i):
                for u in range(UNROLL):
                    at = i * UNROLL + u
                    group[g, pl.ds(at, 1), :] = part[pl.ds(idx[base + g, 0, at] % units, 1), :]

            @pl.when(jnp.logical_and(z == 0, d > 0))
            def _():
                @pl.when(j > 0)
                def _():
                    pl.semaphore_wait(credit_u, 1)

                up_copy((last - d) * ncol + cc).start()

            @pl.when(jnp.logical_and(z == last, d < last))
            def _():
                @pl.when(j > 0)
                def _():
                    pl.semaphore_wait(credit_d, 1)

                down_copy(g).start()

        @pl.when(j < nrow - 1)
        def _():
            load_amps(j + 1)

        @pl.loop(0, nsl)
        def _(s):
            @pl.when(j < nrow - 1)
            def _():
                dots(s)

            @pl.when(s >= lag)
            def _():
                @pl.loop(0, per)
                def _(i):
                    step(j, (s - lag) * per + i)

    @pl.loop(0, nblk)
    def _(g):
        wait_sent(g)

    for k in range(1, ncol):
        amps_copy(k).wait_send()

    @pl.loop(0, nblk)
    def _(n):
        cc = n % ncol

        @pl.when(cc == c)
        def _():
            places_local(n // ncol).wait()

        @pl.when(cc != c)
        def _():
            places_remote(n // ncol, cc).wait_send()
            pltpu.make_async_copy(oall.at[0], gotp.at[n], p_r.at[n]).wait()
            pltpu.make_async_copy(group.at[0], got.at[n], f_r.at[n]).wait()


def exchange(amps, integrals, mask, keys, nrow, ncol):
    arows, depth = amps.shape
    cols = integrals.shape[1]
    nblk = nrow * ncol
    rows = arows * ncol // nrow
    units = rows * cols // TILE
    cap = units // nblk
    nsl = cols // SLICE
    nk = (nrow - 1) * ncol
    any_spec = pl.BlockSpec(memory_space=pl.ANY)
    dma = pltpu.SemaphoreType.DMA
    got, gotp, _, _ = pl.pallas_call(
        functools.partial(exchange_kernel, nrow, ncol),
        out_shape=[
            jax.ShapeDtypeStruct((nblk, cap, TILE), F32),
            jax.ShapeDtypeStruct((nblk, 1, cap), jnp.int32),
            jax.ShapeDtypeStruct((ncol, arows, depth), F32),
            jax.ShapeDtypeStruct((nrow * nblk, 1, cap), jnp.int32),
        ],
        in_specs=[pl.BlockSpec(memory_space=pltpu.SMEM), any_spec, any_spec, any_spec],
        out_specs=[any_spec] * 4,
        scratch_shapes=[
            pltpu.VMEM((2, depth, SLICE), F32),
            pltpu.VMEM((2, arows, depth), F32),
            pltpu.VMEM((rows, depth), BF16),
            pltpu.VMEM((rows, depth), BF16),
            pltpu.VMEM((nsl, depth, SLICE), BF16),
            pltpu.VMEM((nsl, depth, SLICE), BF16),
            pltpu.VMEM((units, TILE), F32),
            pltpu.VMEM((nblk, cap, TILE), F32),
            pltpu.VMEM((nk, cap, TILE), F32),
            pltpu.VMEM((nk, cap, TILE), F32),
            pltpu.SMEM((nrow * nblk, 1, cap), jnp.int32),
            dma((ncol,)), dma((ncol,)), dma((nrow,)), dma((nrow,)), dma((nblk,)), dma((nblk,)),
            dma((nk,)), dma((nk,)), dma((nk,)), dma((nk,)), dma((ncol,)), dma((nblk,)),
            dma((2,)), dma((3,)),
            pltpu.SemaphoreType.REGULAR, pltpu.SemaphoreType.REGULAR,
        ],
        compiler_params=pltpu.CompilerParams(
            collective_id=0, has_side_effects=True, vmem_limit_bytes=62 * 2**20),
        name="exchange",
    )(mask, amps, integrals, keys)
    return got, gotp


def place_kernel(units, tpb, key_ref, mask_ref, got_ref, den_ref, cyc_ref, upd_ref, term_ref, moved, c_hi, c_lo):
    rows = den_ref.shape[0]
    nblk, cap = got_ref.shape[0], got_ref.shape[1]
    k = pl.program_id(0)

    @pl.when(k == 0)
    def _():
        @pl.loop(0, nblk)
        def _(n):
            @pl.loop(0, cap // UNROLL)
            def _(i):
                for u in range(UNROLL):
                    at = i * UNROLL + u
                    q = key_ref[n, 0, at] // units % units
                    moved[pl.ds(q, 1), :] = got_ref[n, pl.ds(at, 1), :]

    for u in range(tpb):
        for s in range(tpb):
            at = (pl.ds(u * TILE, TILE), pl.ds(s * TILE, TILE))
            hi, lo = split(cyc_ref[at] * mask_ref[k * tpb + u, s].astype(F32))
            c_hi[at] = hi
            c_lo[at] = lo
    tiles = [moved[pl.ds(pl.multiple_of((k * tpb + t) * rows, rows), rows), :] for t in range(tpb)]
    upd = jnp.concatenate(tiles, axis=1) / den_ref[...]
    upd_ref[...] = upd
    hi, lo = split(upd)
    term_ref[...] = dot(hi, c_hi[...]) + dot(lo, c_hi[...]) + dot(hi, c_lo[...])


def place(got, gotp, denominators, cycle_tiles, cycle_mask):
    rows, cols = denominators.shape
    rb = cycle_tiles.shape[1]
    units = rows * cols // TILE
    out = jax.ShapeDtypeStruct((rows, cols), F32)
    block = pl.BlockSpec((rows, rb), lambda i, s, m: (0, i))
    return pl.pallas_call(
        functools.partial(place_kernel, units, rb // TILE),
        out_shape=[out, out],
        grid_spec=pltpu.PrefetchScalarGridSpec(
            num_scalar_prefetch=2,
            grid=(cols // rb,),
            in_specs=[
                pl.BlockSpec(got.shape, lambda i, s, m: (0, 0, 0), pipeline_mode=pl.Buffered(1)),
                block,
                pl.BlockSpec((rb, rb), lambda i, s, m: (i, 0)),
            ],
            out_specs=[block, block],
            scratch_shapes=[
                pltpu.VMEM((units, TILE), F32),
                pltpu.VMEM((rb, rb), BF16),
                pltpu.VMEM((rb, rb), BF16),
            ],
        ),
        compiler_params=pltpu.CompilerParams(vmem_limit_bytes=40 * 2**20),
        name="place",
    )(gotp, cycle_mask, got, denominators, cycle_tiles)


def sorted_keys(destination, nrow, ncol):
    rows, tiles = destination.shape
    vt = tiles * ncol
    units = rows * tiles
    flat = destination.T.reshape(-1)
    out_row = flat // vt
    out_tile = flat % vt
    owner = out_row // rows * ncol + out_tile // tiles
    spot = out_tile % tiles * rows + out_row % rows
    key = (owner * units + spot) * units + lax.iota(jnp.int32, units)
    ndev = nrow * ncol
    return lax.sort(key, is_stable=False).reshape(ndev, 1, units // ndev)


def direct(amplitudes, integrals, integral_mask, denominators, cycle_tiles, cycle_mask, destination):
    nrow = lax.axis_size("row")
    ncol = lax.axis_size("col")
    keys = sorted_keys(destination, nrow, ncol)
    got, gotp = exchange(amplitudes, integrals, integral_mask, keys, nrow, ncol)
    return tuple(place(got, gotp, denominators, cycle_tiles, cycle_mask))


def solution(mesh):
    step = direct if (mesh.shape["row"], mesh.shape["col"]) == (4, 8) else body
    return jax.shard_map(
        step,
        mesh=mesh,
        in_specs=(
            P("col", "row"),
            P("row", "col"),
            P("row", "col"),
            P("row", "col"),
            P("col", None),
            P("col", None),
            P("row", "col"),
        ),
        out_specs=(P("row", "col"), P("row", "col")),
        check_vma=False,
    )
```

```python
import functools
import jax
import jax.numpy as jnp
from jax import lax
from jax.experimental import pallas as pl
from jax.experimental.pallas import tpu as pltpu
from jax.sharding import PartitionSpec as P

TILE = 128
F32 = jnp.float32
BF16 = jnp.bfloat16
CHUNKS = 4


def split(x):
    hi = x.astype(BF16)
    return hi, (x - hi.astype(F32)).astype(BF16)


def dot(a, b):
    return jnp.dot(a, b, preferred_element_type=F32)


def product_kernel(nblk, first_tile, tpb, off_ref, mask_ref, a_ref, b_ref, *rest):
    outs, (a_hi, a_lo, b_hi, b_lo) = rest[:-4], rest[-4:]
    rows, depth = a_ref.shape
    blk = rows // nblk
    step = pl.program_id(0)

    @pl.when(step == 0)
    def _():
        for j in range(nblk):
            src = pl.multiple_of(off_ref[j] * blk, blk)
            hi, lo = split(a_ref[pl.ds(src, blk), :])
            a_hi[pl.ds(j * blk, blk), :] = hi
            a_lo[pl.ds(j * blk, blk), :] = lo

    @pl.loop(0, depth // TILE)
    def _(c):
        at = pl.ds(pl.multiple_of(c * TILE, TILE), TILE)
        for t in range(tpb):
            cols = pl.ds(t * TILE, TILE)
            m = mask_ref[c, first_tile + step * tpb + t].astype(F32)
            hi, lo = split(b_ref[at, cols] * m)
            b_hi[at, cols] = hi
            b_lo[at, cols] = lo

    big = rows // 2
    piece = rows // len(outs)
    per = big // piece if big >= piece else 1
    for h in range(2):
        at = pl.ds(h * big, big)
        acc = dot(a_hi[at, :], b_hi[...]) + dot(a_lo[at, :], b_hi[...]) + dot(a_hi[at, :], b_lo[...])
        for t in range(tpb):
            col = acc[:, t * TILE:(t + 1) * TILE]
            if len(outs) == 1:
                outs[0][t, at, :] = col
            else:
                for q in range(per):
                    outs[h * per + q][t, :, :] = col[q * piece:(q + 1) * piece]


def product(amps, integrals, mask, offsets, chunk, nblk, npieces):
    rows, depth = amps.shape
    cols = integrals.shape[1]
    width = cols // CHUNKS
    tpb = min(4, width // TILE)
    bn = tpb * TILE
    steps = width // bn
    piece = rows // npieces
    out = jax.ShapeDtypeStruct((width // TILE, piece, TILE), F32)
    return pl.pallas_call(
        functools.partial(product_kernel, nblk, chunk * (width // TILE), tpb),
        out_shape=[out] * npieces,
        grid_spec=pltpu.PrefetchScalarGridSpec(
            num_scalar_prefetch=2,
            grid=(steps,),
            in_specs=[
                pl.BlockSpec((rows, depth), lambda i, o, m: (0, 0), pipeline_mode=pl.Buffered(1)),
                pl.BlockSpec((depth, bn), lambda i, o, m: (0, chunk * steps + i)),
            ],
            out_specs=[pl.BlockSpec((tpb, piece, TILE), lambda i, o, m: (i, 0, 0))] * npieces,
            scratch_shapes=[
                pltpu.VMEM((rows, depth), BF16),
                pltpu.VMEM((rows, depth), BF16),
                pltpu.VMEM((depth, bn), BF16),
                pltpu.VMEM((depth, bn), BF16),
            ],
        ),
        cost_estimate=pl.CostEstimate(
            flops=6 * rows * depth * width,
            bytes_accessed=4 * (rows * depth + depth * width + rows * width),
            transcendentals=0,
        ),
        compiler_params=pltpu.CompilerParams(vmem_limit_bytes=56 * 2**20),
        name="product",
    )(offsets, mask, amps, integrals)


def gather_kernel(idx_ref, x_ref, o_ref):
    n = o_ref.shape[0]
    base = pl.program_id(0) * n

    @pl.loop(0, n // 16)
    def _(i):
        for u in range(16):
            k = i * 16 + u
            o_ref[pl.ds(k, 1), :] = x_ref[pl.ds(idx_ref[base + k], 1), :]


def gather_units(units, idx):
    n = units.shape[0]
    bn = min(1024, n)
    return pl.pallas_call(
        gather_kernel,
        out_shape=jax.ShapeDtypeStruct(units.shape, F32),
        grid_spec=pltpu.PrefetchScalarGridSpec(
            num_scalar_prefetch=1,
            grid=(n // bn,),
            in_specs=[pl.BlockSpec(units.shape, lambda i, s: (0, 0), pipeline_mode=pl.Buffered(1))],
            out_specs=pl.BlockSpec((bn, TILE), lambda i, s: (i, 0)),
        ),
        compiler_params=pltpu.CompilerParams(vmem_limit_bytes=24 * 2**20),
        name="gather_units",
    )(idx, units)


def finish_kernel(tiles, tpb, idx_ref, mask_ref, got_ref, den_ref, cyc_ref, upd_ref, term_ref, moved, c_hi, c_lo):
    rows = den_ref.shape[0]
    k = pl.program_id(0)

    @pl.loop(0, rows // 8)
    def _(i):
        for u in range(8):
            r = i * 8 + u
            for t in range(tpb):
                q = idx_ref[r * tiles + k * tpb + t]
                moved[t, pl.ds(r, 1), :] = got_ref[pl.ds(q, 1), :]

    for u in range(tpb):
        for s in range(tpb):
            at = (pl.ds(u * TILE, TILE), pl.ds(s * TILE, TILE))
            hi, lo = split(cyc_ref[at] * mask_ref[k * tpb + u, s].astype(F32))
            c_hi[at] = hi
            c_lo[at] = lo
    upd = jnp.concatenate([moved[t] for t in range(tpb)], axis=1) / den_ref[...]
    upd_ref[...] = upd
    hi, lo = split(upd)
    term_ref[...] = dot(hi, c_hi[...]) + dot(lo, c_hi[...]) + dot(hi, c_lo[...])


def finish(got, inv, denominators, cycle_tiles, cycle_mask):
    rows, cols = denominators.shape
    rb = cycle_tiles.shape[1]
    out = jax.ShapeDtypeStruct((rows, cols), F32)
    block = pl.BlockSpec((rows, rb), lambda i, s, m: (0, i))
    return pl.pallas_call(
        functools.partial(finish_kernel, cols // TILE, rb // TILE),
        out_shape=[out, out],
        grid_spec=pltpu.PrefetchScalarGridSpec(
            num_scalar_prefetch=2,
            grid=(cols // rb,),
            in_specs=[
                pl.BlockSpec(got.shape, lambda i, s, m: (0, 0), pipeline_mode=pl.Buffered(1)),
                block,
                pl.BlockSpec((rb, rb), lambda i, s, m: (i, 0)),
            ],
            out_specs=[block, block],
            scratch_shapes=[
                pltpu.VMEM((rb // TILE, rows, TILE), F32),
                pltpu.VMEM((rb, rb), BF16),
                pltpu.VMEM((rb, rb), BF16),
            ],
        ),
        compiler_params=pltpu.CompilerParams(vmem_limit_bytes=40 * 2**20),
        name="finish",
    )(inv, cycle_mask, got, denominators, cycle_tiles)


def routes(destination, nrow, ncol):
    local_rows, local_tiles = destination.shape
    vt = local_tiles * ncol
    units = local_rows * local_tiles
    half = local_rows // 2
    tc = local_tiles // CHUNKS
    flat = destination.reshape(2, half, CHUNKS, tc).transpose(2, 0, 3, 1).reshape(-1)
    out_row = flat // vt
    out_tile = flat % vt
    owner = out_row // local_rows * ncol + out_tile // local_tiles
    place = out_row % local_rows * local_tiles + out_tile % local_tiles
    iota = lax.iota(jnp.int32, units)
    key, order = lax.sort((owner * units + place, iota), num_keys=1, is_stable=False)
    ndev = nrow * ncol
    places = (key % units).astype(F32).reshape(ndev, units // ndev)
    got_place = lax.all_to_all(places, ("row", "col"), split_axis=0, concat_axis=0, tiled=True)
    _, inv = lax.sort((got_place.reshape(-1).astype(jnp.int32), iota), num_keys=1, is_stable=False)
    return order, inv


def body(amplitudes, integrals, integral_mask, denominators, cycle_tiles, cycle_mask, destination):
    nrow = lax.axis_size("row")
    ncol = lax.axis_size("col")
    me = lax.axis_index("row")
    amps = lax.all_gather(amplitudes, "col", axis=0, tiled=True)
    order, inv = routes(destination, nrow, ncol)
    local_rows = destination.shape[0]
    half = local_rows // 2
    pieces = []
    if nrow == 4:
        up = [(i, (i + 1) % nrow) for i in range(nrow)]
        down = [(i, (i - 1) % nrow) for i in range(nrow)]
        offsets = jnp.stack([(me + d) % nrow for d in (2, 1, 3, 0)]).astype(jnp.int32)
        sent, landed = [], []
        for c in range(CHUNKS):
            if c >= 2:
                after = sent[c - 2] + (landed[c - 3] if c >= 3 else [])
                offsets = lax.optimization_barrier([offsets] + after)[0]
            far_a, far_b, up_a, up_b, dn_a, dn_b, own_a, own_b = product(
                amps, integrals, integral_mask, offsets, c, nrow, 2 * nrow)
            in_a = lax.ppermute(far_a, "row", up)
            in_b = lax.ppermute(far_b, "row", down)
            direct_b = lax.ppermute(up_b, "row", up)
            direct_a = lax.ppermute(dn_a, "row", down)
            next_a, next_b = up_a + in_a, dn_b + in_b
            sum_a = lax.ppermute(next_a, "row", up)
            sum_b = lax.ppermute(next_b, "row", down)
            sent.append([next_a, next_b, direct_a, direct_b])
            landed.append([sum_a, sum_b])
            pieces.append(own_a + direct_a + sum_a)
            pieces.append(own_b + direct_b + sum_b)
    else:
        offsets = lax.iota(jnp.int32, nrow)
        for c in range(CHUNKS):
            (part,) = product(amps, integrals, integral_mask, offsets, c, nrow, 1)
            summed = lax.psum_scatter(part, "row", scatter_dimension=1, tiled=True)
            pieces.append(summed[:, :half])
            pieces.append(summed[:, half:])
    units = jnp.concatenate([p.reshape(-1, TILE) for p in pieces], axis=0)
    sending = gather_units(units, order)
    ndev = nrow * ncol
    got = lax.all_to_all(sending.reshape(ndev, -1, TILE), ("row", "col"), split_axis=0, concat_axis=0, tiled=True)
    return tuple(finish(got.reshape(-1, TILE), inv, denominators, cycle_tiles, cycle_mask))


MESH = pl.DeviceIdType.MESH
SLICE = 512
UNROLL = 16
LAG = 4


def exchange_kernel(nrow, ncol, mask_ref, amps, integ, order, spots, got, gotp, aall, oall, pall,
                    st, ast, ah, al, bh, bl, part, group, ru, rd, idx,
                    a_s, a_r, o_s, o_r, q_s, q_r, p_s, p_r, u_s, u_r, d_s, d_r, f_s, f_r, b_sem, l_sem, credit_u, credit_d):
    z = lax.axis_index("row")
    c = lax.axis_index("col")
    last = nrow - 1
    arows, depth = amps.shape
    nblk, cap = got.shape[0], got.shape[1]
    units = nblk * cap
    nsl, _, width = bh.shape
    tps = width // TILE
    rows = ah.shape[0]
    nk = last * ncol
    low = 1 - z // 2
    core = c % 2
    cx = c // 2 % 2
    cy = c // 4

    def peer(k):
        px = (cx + k // 2 % 2) % 2
        py = (cy + k // 4) % 2
        return (py * 2 + px) * 2 + (core + k % 2) % 2

    def block_of(j):
        return (cy + j // 2) % 2 * 2 + (cx + j % 2) % 2

    def amps_copy(k):
        return pltpu.make_async_remote_copy(amps, aall.at[c], a_s.at[k], a_r.at[k], (z, peer(k)), MESH)

    def order_copy(dz):
        at = pl.ds(pl.multiple_of(z * units, units), units)
        return pltpu.make_async_remote_copy(order, oall.at[at], o_s.at[dz], o_r.at[dz], ((z + dz) % nrow, c), MESH)

    def spots_copy(dz):
        return pltpu.make_async_remote_copy(
            spots, pall.at[pl.ds(z * nblk, nblk)], q_s.at[dz], q_r.at[dz], ((z + dz) % nrow, c), MESH)

    def up_copy(k):
        g = (last - k // ncol) * ncol + k % ncol
        return pltpu.make_async_remote_copy(group.at[g], ru.at[k], u_s.at[k], u_r.at[k], ((z + 1) % nrow, c), MESH)

    def down_copy(k):
        return pltpu.make_async_remote_copy(
            group.at[k], rd.at[k], d_s.at[k], d_r.at[k], ((z + nrow - 1) % nrow, c), MESH)

    def final_copy(j, cc):
        s = block_of(j) * ncol + c
        return pltpu.make_async_remote_copy(group.at[z * ncol + cc], got.at[s], f_s.at[cc], f_r.at[s], (z, cc), MESH)

    def final_local(j):
        return pltpu.make_async_copy(group.at[z * ncol + c], got.at[block_of(j) * ncol + c], f_s.at[c])

    def load_cols(s, slot):
        at = pl.ds(pl.multiple_of(s * width, width), width)
        return pltpu.make_async_copy(integ.at[:, at], st.at[slot], b_sem.at[slot])

    def load_amps(j):
        r = block_of(j)
        for i in range(2):
            e = (i + core) % 2
            dst, sem = ast.at[i], l_sem.at[i]
            own = (j + e) == 0

            @pl.when(own)
            def _():
                pltpu.make_async_copy(amps, dst, sem).start()

            @pl.when(jnp.logical_not(own))
            def _():
                amps_copy(j * 2 + e).wait_recv()
                pltpu.make_async_copy(aall.at[r * 2 + i], dst, sem).start()

        for i in range(2):
            pltpu.make_async_copy(amps, ast.at[i], l_sem.at[i]).wait()

            @pl.loop(0, arows // 16)
            def _(n):
                at = pl.ds(pl.multiple_of(n * 16, 16), 16)
                to = pl.ds(pl.multiple_of(i * arows + n * 16, 16), 16)
                hi, lo = split(ast[i, at, :])
                ah[to, :] = hi
                al[to, :] = lo

    def dots(s):
        acc = dot(ah[...], bh[s]) + dot(al[...], bh[s]) + dot(ah[...], bl[s])
        for t in range(tps):
            at = pl.ds(pl.multiple_of((s * tps + t) * rows, rows), rows)
            part[at, :] = acc[:, t * TILE:(t + 1) * TILE]

    def split_cols(s, slot):
        @pl.loop(0, depth // TILE)
        def _(n):
            at = pl.ds(pl.multiple_of(n * TILE, TILE), TILE)
            for t in range(tps):
                cols = pl.ds(t * TILE, TILE)
                hi, lo = split(st[slot, at, cols] * mask_ref[n, s * tps + t].astype(F32))
                bh[s, at, cols] = hi
                bl[s, at, cols] = lo

    for slot in range(2):
        load_cols(slot, slot).start()
    barrier = pltpu.get_barrier_semaphore()
    for k in range(1, ncol):
        pl.semaphore_signal(barrier, 1, device_id=(z, peer(k)), device_id_type=MESH)
    for dz in range(1, nrow):
        pl.semaphore_signal(barrier, 1, device_id=((z + dz) % nrow, c), device_id_type=MESH)
    pl.semaphore_wait(barrier, ncol - 1 + nrow - 1)

    for dz in range(1, nrow):
        order_copy(dz).start()
        spots_copy(dz).start()
    for k in range(1, ncol):
        amps_copy(k).start()
    own_order = pltpu.make_async_copy(order, oall.at[pl.ds(pl.multiple_of(z * units, units), units)], l_sem.at[2])
    own_order.start()
    own_spots = pltpu.make_async_copy(spots, pall.at[pl.ds(z * nblk, nblk)], l_sem.at[3])
    own_spots.start()

    load_amps(0)

    @pl.loop(0, nsl)
    def _(s):
        slot = s % 2
        load_cols(s, slot).wait()
        split_cols(s, slot)

        @pl.when(s < nsl - 2)
        def _():
            load_cols(s + 2, slot).start()

        dots(s)

    own_order.wait()
    own_spots.wait()
    for dz in range(1, nrow):
        order_copy(dz).wait()
        spots_copy(dz).wait()
    to_scalar = pltpu.make_async_copy(oall, idx, l_sem.at[2])
    to_scalar.start()

    def places_remote(r, cc):
        return pltpu.make_async_remote_copy(
            pall.at[r * nblk + z * ncol + cc], gotp.at[r * ncol + c], p_s.at[r * ncol + cc], p_r.at[r * ncol + c],
            (z, cc), MESH)

    def places_local(r):
        return pltpu.make_async_copy(pall.at[r * nblk + z * ncol + c], gotp.at[r * ncol + c], p_s.at[r * ncol + c])

    @pl.loop(0, nblk)
    def _(n):
        r = n // ncol
        cc = n % ncol

        @pl.when(cc == c)
        def _():
            places_local(r).start()

        @pl.when(cc != c)
        def _():
            places_remote(r, cc).start()

    to_scalar.wait()

    def step(j, k):
        more = j < nrow - 1
        ku = k - (1 - low) * LAG
        kd = k - low * LAG
        d = last - ku // ncol

        @pl.when(jnp.logical_and(jnp.logical_and(z >= 1, ku >= 0), d >= z))
        def _():
            up_copy(ku).wait_recv()
            group[d * ncol + ku % ncol] += ru[ku]

            @pl.when(more)
            def _():
                pl.semaphore_signal(credit_u, 1, device_id=((z + nrow - 1) % nrow, c), device_id_type=MESH)

            @pl.when(d > z)
            def _():
                @pl.when(j > 0)
                def _():
                    pl.semaphore_wait(credit_u, 1)

                up_copy(ku).start()

        e = kd // ncol

        @pl.when(jnp.logical_and(jnp.logical_and(z < last, kd >= 0), e <= z))
        def _():
            down_copy(kd).wait_recv()
            group[kd] += rd[kd]

            @pl.when(more)
            def _():
                pl.semaphore_signal(credit_d, 1, device_id=((z + 1) % nrow, c), device_id_type=MESH)

            @pl.when(e < z)
            def _():
                @pl.when(j > 0)
                def _():
                    pl.semaphore_wait(credit_d, 1)

                down_copy(kd).start()

        inner = z * (last - z)
        kf = k - (1 - (inner + 1) // 2) * LAG + ncol
        cc = kf % ncol

        @pl.when(kf // ncol == inner + 1)
        def _():
            @pl.when(cc == c)
            def _():
                final_local(j).start()

            @pl.when(cc != c)
            def _():
                final_copy(j, cc).start()

    def wait_sent(g):
        d = g // ncol
        cc = g % ncol

        @pl.when(d > z)
        def _():
            up_copy((last - d) * ncol + cc).wait_send()

        @pl.when(d < z)
        def _():
            down_copy(g).wait_send()

        @pl.when(jnp.logical_and(d == z, cc == c))
        def _():
            final_local(0).wait()

        @pl.when(jnp.logical_and(d == z, cc != c))
        def _():
            final_copy(0, cc).wait_send()

    lag = 2
    per = nk // (nsl - lag)

    @pl.loop(0, nrow)
    def _(j):
        base = block_of(j) * units

        @pl.loop(0, nblk)
        def _(n):
            q = n // ncol
            cc = n % ncol
            d = low * (last - q) + (1 - low) * q
            g = d * ncol + cc

            @pl.when(j > 0)
            def _():
                wait_sent(g)

            @pl.loop(0, cap // UNROLL)
            def _(i):
                first = base + g * cap + i * UNROLL
                for u in range(UNROLL):
                    group[g, pl.ds(i * UNROLL + u, 1), :] = part[pl.ds(idx[first + u], 1), :]

            @pl.when(jnp.logical_and(z == 0, d > 0))
            def _():
                @pl.when(j > 0)
                def _():
                    pl.semaphore_wait(credit_u, 1)

                up_copy((last - d) * ncol + cc).start()

            @pl.when(jnp.logical_and(z == last, d < last))
            def _():
                @pl.when(j > 0)
                def _():
                    pl.semaphore_wait(credit_d, 1)

                down_copy(g).start()

        @pl.when(j < nrow - 1)
        def _():
            load_amps(j + 1)

        @pl.loop(0, nsl)
        def _(s):
            @pl.when(j < nrow - 1)
            def _():
                dots(s)

            @pl.when(s >= lag)
            def _():
                @pl.loop(0, per)
                def _(i):
                    step(j, (s - lag) * per + i)

    @pl.loop(0, nblk)
    def _(g):
        wait_sent(g)

    for k in range(1, ncol):
        amps_copy(k).wait_send()

    @pl.loop(0, nblk)
    def _(n):
        cc = n % ncol

        @pl.when(cc == c)
        def _():
            places_local(n // ncol).wait()

        @pl.when(cc != c)
        def _():
            places_remote(n // ncol, cc).wait_send()
            pltpu.make_async_copy(pall.at[0], gotp.at[n], p_r.at[n]).wait()
            pltpu.make_async_copy(group.at[0], got.at[n], f_r.at[n]).wait()


def exchange(amps, integrals, mask, order, spots, nrow, ncol):
    arows, depth = amps.shape
    cols = integrals.shape[1]
    nblk = nrow * ncol
    rows = arows * ncol // nrow
    units = rows * cols // TILE
    cap = units // nblk
    nsl = cols // SLICE
    nk = (nrow - 1) * ncol
    any_spec = pl.BlockSpec(memory_space=pl.ANY)
    dma = pltpu.SemaphoreType.DMA
    got, gotp, _, _, _ = pl.pallas_call(
        functools.partial(exchange_kernel, nrow, ncol),
        out_shape=[
            jax.ShapeDtypeStruct((nblk, cap, TILE), F32),
            jax.ShapeDtypeStruct((nblk, 1, cap), jnp.int32),
            jax.ShapeDtypeStruct((ncol, arows, depth), F32),
            jax.ShapeDtypeStruct((nrow * units,), jnp.int32),
            jax.ShapeDtypeStruct((nrow * nblk, 1, cap), jnp.int32),
        ],
        in_specs=[pl.BlockSpec(memory_space=pltpu.SMEM)] + [any_spec] * 4,
        out_specs=[any_spec] * 5,
        scratch_shapes=[
            pltpu.VMEM((2, depth, SLICE), F32),
            pltpu.VMEM((2, arows, depth), F32),
            pltpu.VMEM((rows, depth), BF16),
            pltpu.VMEM((rows, depth), BF16),
            pltpu.VMEM((nsl, depth, SLICE), BF16),
            pltpu.VMEM((nsl, depth, SLICE), BF16),
            pltpu.VMEM((units, TILE), F32),
            pltpu.VMEM((nblk, cap, TILE), F32),
            pltpu.VMEM((nk, cap, TILE), F32),
            pltpu.VMEM((nk, cap, TILE), F32),
            pltpu.SMEM((nrow * units,), jnp.int32),
            dma((ncol,)), dma((ncol,)), dma((nrow,)), dma((nrow,)), dma((nrow,)), dma((nrow,)),
            dma((nblk,)), dma((nblk,)),
            dma((nk,)), dma((nk,)), dma((nk,)), dma((nk,)), dma((ncol,)), dma((nblk,)),
            dma((2,)), dma((4,)),
            pltpu.SemaphoreType.REGULAR, pltpu.SemaphoreType.REGULAR,
        ],
        compiler_params=pltpu.CompilerParams(
            collective_id=0, has_side_effects=True, vmem_limit_bytes=62 * 2**20),
        name="exchange",
    )(mask, amps, integrals, order, spots)
    return got, gotp


def place_kernel(tpb, spot_ref, mask_ref, got_ref, den_ref, cyc_ref, upd_ref, term_ref, moved, c_hi, c_lo):
    rows = den_ref.shape[0]
    nblk, cap = got_ref.shape[0], got_ref.shape[1]
    k = pl.program_id(0)

    @pl.when(k == 0)
    def _():
        @pl.loop(0, nblk)
        def _(n):
            @pl.loop(0, cap // UNROLL)
            def _(i):
                first = n * cap + i * UNROLL
                for u in range(UNROLL):
                    moved[pl.ds(spot_ref[first + u], 1), :] = got_ref[n, pl.ds(i * UNROLL + u, 1), :]

    for u in range(tpb):
        for s in range(tpb):
            at = (pl.ds(u * TILE, TILE), pl.ds(s * TILE, TILE))
            hi, lo = split(cyc_ref[at] * mask_ref[k * tpb + u, s].astype(F32))
            c_hi[at] = hi
            c_lo[at] = lo
    tiles = [moved[pl.ds(pl.multiple_of((k * tpb + t) * rows, rows), rows), :] for t in range(tpb)]
    upd = jnp.concatenate(tiles, axis=1) / den_ref[...]
    upd_ref[...] = upd
    hi, lo = split(upd)
    term_ref[...] = dot(hi, c_hi[...]) + dot(lo, c_hi[...]) + dot(hi, c_lo[...])


def place(got, gotp, denominators, cycle_tiles, cycle_mask):
    rows, cols = denominators.shape
    rb = cycle_tiles.shape[1]
    units = rows * cols // TILE
    out = jax.ShapeDtypeStruct((rows, cols), F32)
    block = pl.BlockSpec((rows, rb), lambda i, s, m: (0, i))
    return pl.pallas_call(
        functools.partial(place_kernel, rb // TILE),
        out_shape=[out, out],
        grid_spec=pltpu.PrefetchScalarGridSpec(
            num_scalar_prefetch=2,
            grid=(cols // rb,),
            in_specs=[
                pl.BlockSpec(got.shape, lambda i, s, m: (0, 0, 0), pipeline_mode=pl.Buffered(1)),
                block,
                pl.BlockSpec((rb, rb), lambda i, s, m: (i, 0)),
            ],
            out_specs=[block, block],
            scratch_shapes=[
                pltpu.VMEM((units, TILE), F32),
                pltpu.VMEM((rb, rb), BF16),
                pltpu.VMEM((rb, rb), BF16),
            ],
        ),
        compiler_params=pltpu.CompilerParams(vmem_limit_bytes=62 * 2**20),
        name="place",
    )(gotp.reshape(-1), cycle_mask, got, denominators, cycle_tiles)


def sorted_keys(destination, nrow, ncol):
    rows, tiles = destination.shape
    vt = tiles * ncol
    units = rows * tiles
    flat = destination.T.reshape(-1)
    out_row = flat // vt
    out_tile = flat % vt
    owner = out_row // rows * ncol + out_tile // tiles
    spot = out_tile % tiles * rows + out_row % rows
    key = (owner * units + spot) * units + lax.iota(jnp.int32, units)
    ndev = nrow * ncol
    key = lax.sort(key, is_stable=False)
    return key % units, (key // units % units).reshape(ndev, 1, units // ndev)


def direct(amplitudes, integrals, integral_mask, denominators, cycle_tiles, cycle_mask, destination):
    nrow = lax.axis_size("row")
    ncol = lax.axis_size("col")
    order, spots = sorted_keys(destination, nrow, ncol)
    got, gotp = exchange(amplitudes, integrals, integral_mask, order, spots, nrow, ncol)
    return tuple(place(got, gotp, denominators, cycle_tiles, cycle_mask))


def solution(mesh):
    step = direct if (mesh.shape["row"], mesh.shape["col"]) == (4, 8) else body
    return jax.shard_map(
        step,
        mesh=mesh,
        in_specs=(
            P("col", "row"),
            P("row", "col"),
            P("row", "col"),
            P("row", "col"),
            P("col", None),
            P("col", None),
            P("row", "col"),
        ),
        out_specs=(P("row", "col"), P("row", "col")),
        check_vma=False,
    )
```

```python
import functools
import jax
import jax.numpy as jnp
from jax import lax
from jax.experimental import pallas as pl
from jax.experimental.pallas import tpu as pltpu
from jax.sharding import PartitionSpec as P

TILE = 128
F32 = jnp.float32
BF16 = jnp.bfloat16
CHUNKS = 4


def split(x):
    hi = x.astype(BF16)
    return hi, (x - hi.astype(F32)).astype(BF16)


def dot(a, b):
    return jnp.dot(a, b, preferred_element_type=F32)


def product_kernel(nblk, first_tile, tpb, off_ref, mask_ref, a_ref, b_ref, *rest):
    outs, (a_hi, a_lo, b_hi, b_lo) = rest[:-4], rest[-4:]
    rows, depth = a_ref.shape
    blk = rows // nblk
    step = pl.program_id(0)

    @pl.when(step == 0)
    def _():
        for j in range(nblk):
            src = pl.multiple_of(off_ref[j] * blk, blk)
            hi, lo = split(a_ref[pl.ds(src, blk), :])
            a_hi[pl.ds(j * blk, blk), :] = hi
            a_lo[pl.ds(j * blk, blk), :] = lo

    @pl.loop(0, depth // TILE)
    def _(c):
        at = pl.ds(pl.multiple_of(c * TILE, TILE), TILE)
        for t in range(tpb):
            cols = pl.ds(t * TILE, TILE)
            m = mask_ref[c, first_tile + step * tpb + t].astype(F32)
            hi, lo = split(b_ref[at, cols] * m)
            b_hi[at, cols] = hi
            b_lo[at, cols] = lo

    big = rows // 2
    piece = rows // len(outs)
    per = big // piece if big >= piece else 1
    for h in range(2):
        at = pl.ds(h * big, big)
        acc = dot(a_hi[at, :], b_hi[...]) + dot(a_lo[at, :], b_hi[...]) + dot(a_hi[at, :], b_lo[...])
        for t in range(tpb):
            col = acc[:, t * TILE:(t + 1) * TILE]
            if len(outs) == 1:
                outs[0][t, at, :] = col
            else:
                for q in range(per):
                    outs[h * per + q][t, :, :] = col[q * piece:(q + 1) * piece]


def product(amps, integrals, mask, offsets, chunk, nblk, npieces):
    rows, depth = amps.shape
    cols = integrals.shape[1]
    width = cols // CHUNKS
    tpb = min(4, width // TILE)
    bn = tpb * TILE
    steps = width // bn
    piece = rows // npieces
    out = jax.ShapeDtypeStruct((width // TILE, piece, TILE), F32)
    return pl.pallas_call(
        functools.partial(product_kernel, nblk, chunk * (width // TILE), tpb),
        out_shape=[out] * npieces,
        grid_spec=pltpu.PrefetchScalarGridSpec(
            num_scalar_prefetch=2,
            grid=(steps,),
            in_specs=[
                pl.BlockSpec((rows, depth), lambda i, o, m: (0, 0), pipeline_mode=pl.Buffered(1)),
                pl.BlockSpec((depth, bn), lambda i, o, m: (0, chunk * steps + i)),
            ],
            out_specs=[pl.BlockSpec((tpb, piece, TILE), lambda i, o, m: (i, 0, 0))] * npieces,
            scratch_shapes=[
                pltpu.VMEM((rows, depth), BF16),
                pltpu.VMEM((rows, depth), BF16),
                pltpu.VMEM((depth, bn), BF16),
                pltpu.VMEM((depth, bn), BF16),
            ],
        ),
        cost_estimate=pl.CostEstimate(
            flops=6 * rows * depth * width,
            bytes_accessed=4 * (rows * depth + depth * width + rows * width),
            transcendentals=0,
        ),
        compiler_params=pltpu.CompilerParams(vmem_limit_bytes=56 * 2**20),
        name="product",
    )(offsets, mask, amps, integrals)


def gather_kernel(idx_ref, x_ref, o_ref):
    n = o_ref.shape[0]
    base = pl.program_id(0) * n

    @pl.loop(0, n // 16)
    def _(i):
        for u in range(16):
            k = i * 16 + u
            o_ref[pl.ds(k, 1), :] = x_ref[pl.ds(idx_ref[base + k], 1), :]


def gather_units(units, idx):
    n = units.shape[0]
    bn = min(1024, n)
    return pl.pallas_call(
        gather_kernel,
        out_shape=jax.ShapeDtypeStruct(units.shape, F32),
        grid_spec=pltpu.PrefetchScalarGridSpec(
            num_scalar_prefetch=1,
            grid=(n // bn,),
            in_specs=[pl.BlockSpec(units.shape, lambda i, s: (0, 0), pipeline_mode=pl.Buffered(1))],
            out_specs=pl.BlockSpec((bn, TILE), lambda i, s: (i, 0)),
        ),
        compiler_params=pltpu.CompilerParams(vmem_limit_bytes=24 * 2**20),
        name="gather_units",
    )(idx, units)


def finish_kernel(tiles, tpb, idx_ref, mask_ref, got_ref, den_ref, cyc_ref, upd_ref, term_ref, moved, c_hi, c_lo):
    rows = den_ref.shape[0]
    k = pl.program_id(0)

    @pl.loop(0, rows // 8)
    def _(i):
        for u in range(8):
            r = i * 8 + u
            for t in range(tpb):
                q = idx_ref[r * tiles + k * tpb + t]
                moved[t, pl.ds(r, 1), :] = got_ref[pl.ds(q, 1), :]

    for u in range(tpb):
        for s in range(tpb):
            at = (pl.ds(u * TILE, TILE), pl.ds(s * TILE, TILE))
            hi, lo = split(cyc_ref[at] * mask_ref[k * tpb + u, s].astype(F32))
            c_hi[at] = hi
            c_lo[at] = lo
    upd = jnp.concatenate([moved[t] for t in range(tpb)], axis=1) / den_ref[...]
    upd_ref[...] = upd
    hi, lo = split(upd)
    term_ref[...] = dot(hi, c_hi[...]) + dot(lo, c_hi[...]) + dot(hi, c_lo[...])


def finish(got, inv, denominators, cycle_tiles, cycle_mask):
    rows, cols = denominators.shape
    rb = cycle_tiles.shape[1]
    out = jax.ShapeDtypeStruct((rows, cols), F32)
    block = pl.BlockSpec((rows, rb), lambda i, s, m: (0, i))
    return pl.pallas_call(
        functools.partial(finish_kernel, cols // TILE, rb // TILE),
        out_shape=[out, out],
        grid_spec=pltpu.PrefetchScalarGridSpec(
            num_scalar_prefetch=2,
            grid=(cols // rb,),
            in_specs=[
                pl.BlockSpec(got.shape, lambda i, s, m: (0, 0), pipeline_mode=pl.Buffered(1)),
                block,
                pl.BlockSpec((rb, rb), lambda i, s, m: (i, 0)),
            ],
            out_specs=[block, block],
            scratch_shapes=[
                pltpu.VMEM((rb // TILE, rows, TILE), F32),
                pltpu.VMEM((rb, rb), BF16),
                pltpu.VMEM((rb, rb), BF16),
            ],
        ),
        compiler_params=pltpu.CompilerParams(vmem_limit_bytes=40 * 2**20),
        name="finish",
    )(inv, cycle_mask, got, denominators, cycle_tiles)


def routes(destination, nrow, ncol):
    local_rows, local_tiles = destination.shape
    vt = local_tiles * ncol
    units = local_rows * local_tiles
    half = local_rows // 2
    tc = local_tiles // CHUNKS
    flat = destination.reshape(2, half, CHUNKS, tc).transpose(2, 0, 3, 1).reshape(-1)
    out_row = flat // vt
    out_tile = flat % vt
    owner = out_row // local_rows * ncol + out_tile // local_tiles
    place = out_row % local_rows * local_tiles + out_tile % local_tiles
    iota = lax.iota(jnp.int32, units)
    key, order = lax.sort((owner * units + place, iota), num_keys=1, is_stable=False)
    ndev = nrow * ncol
    places = (key % units).astype(F32).reshape(ndev, units // ndev)
    got_place = lax.all_to_all(places, ("row", "col"), split_axis=0, concat_axis=0, tiled=True)
    _, inv = lax.sort((got_place.reshape(-1).astype(jnp.int32), iota), num_keys=1, is_stable=False)
    return order, inv


def body(amplitudes, integrals, integral_mask, denominators, cycle_tiles, cycle_mask, destination):
    nrow = lax.axis_size("row")
    ncol = lax.axis_size("col")
    me = lax.axis_index("row")
    amps = lax.all_gather(amplitudes, "col", axis=0, tiled=True)
    order, inv = routes(destination, nrow, ncol)
    local_rows = destination.shape[0]
    half = local_rows // 2
    pieces = []
    if nrow == 4:
        up = [(i, (i + 1) % nrow) for i in range(nrow)]
        down = [(i, (i - 1) % nrow) for i in range(nrow)]
        offsets = jnp.stack([(me + d) % nrow for d in (2, 1, 3, 0)]).astype(jnp.int32)
        sent, landed = [], []
        for c in range(CHUNKS):
            if c >= 2:
                after = sent[c - 2] + (landed[c - 3] if c >= 3 else [])
                offsets = lax.optimization_barrier([offsets] + after)[0]
            far_a, far_b, up_a, up_b, dn_a, dn_b, own_a, own_b = product(
                amps, integrals, integral_mask, offsets, c, nrow, 2 * nrow)
            in_a = lax.ppermute(far_a, "row", up)
            in_b = lax.ppermute(far_b, "row", down)
            direct_b = lax.ppermute(up_b, "row", up)
            direct_a = lax.ppermute(dn_a, "row", down)
            next_a, next_b = up_a + in_a, dn_b + in_b
            sum_a = lax.ppermute(next_a, "row", up)
            sum_b = lax.ppermute(next_b, "row", down)
            sent.append([next_a, next_b, direct_a, direct_b])
            landed.append([sum_a, sum_b])
            pieces.append(own_a + direct_a + sum_a)
            pieces.append(own_b + direct_b + sum_b)
    else:
        offsets = lax.iota(jnp.int32, nrow)
        for c in range(CHUNKS):
            (part,) = product(amps, integrals, integral_mask, offsets, c, nrow, 1)
            summed = lax.psum_scatter(part, "row", scatter_dimension=1, tiled=True)
            pieces.append(summed[:, :half])
            pieces.append(summed[:, half:])
    units = jnp.concatenate([p.reshape(-1, TILE) for p in pieces], axis=0)
    sending = gather_units(units, order)
    ndev = nrow * ncol
    got = lax.all_to_all(sending.reshape(ndev, -1, TILE), ("row", "col"), split_axis=0, concat_axis=0, tiled=True)
    return tuple(finish(got.reshape(-1, TILE), inv, denominators, cycle_tiles, cycle_mask))


MESH = pl.DeviceIdType.MESH
SLICE = 512
UNROLL = 16
LAG = 4
PORTION = 4


def exchange_kernel(nrow, ncol, mask_ref, amps, integ, order, spots, got, gotp, pre, aall, oall, pall,
                    st, ast, ah, al, bh0, bl0, bh1, bl1, part, group, ru, rd, idx, spot, total, found, inv,
                    a_s, a_r, o_s, o_r, q_s, q_r, p_s, p_r, u_s, u_r, d_s, d_r, f_s, f_r, b_sem, l_sem, credit_u, credit_d):
    z = lax.axis_index("row")
    c = lax.axis_index("col")
    last = nrow - 1
    arows, depth = amps.shape
    nblk, cap = got.shape[0], got.shape[1]
    units = nblk * cap
    half, _, width = bh0.shape
    nsl = half * 2
    bands = (bh0, bl0), (bh1, bl1)
    tps = width // TILE
    rows = ah.shape[0]
    nk = last * ncol
    low = 1 - z // 2
    inner = z * (last - z)
    end = 1 - (inner + 1) // 2
    core = c % 2
    cx = c // 2 % 2
    cy = c // 4

    def peer(k):
        px = (cx + k // 2 % 2) % 2
        py = (cy + k // 4) % 2
        return (py * 2 + px) * 2 + (core + k % 2) % 2

    def col_of(i):
        return peer(ncol - 1 - i)

    def block_of(j):
        return (cy + j // 2) % 2 * 2 + (cx + j % 2) % 2

    def amps_copy(k):
        return pltpu.make_async_remote_copy(amps, aall.at[c], a_s.at[k], a_r.at[k], (z, peer(k)), MESH)

    def order_copy(dz):
        at = pl.ds(pl.multiple_of(z * units, units), units)
        return pltpu.make_async_remote_copy(order, oall.at[at], o_s.at[dz], o_r.at[dz], ((z + dz) % nrow, c), MESH)

    def spots_copy(dz):
        return pltpu.make_async_remote_copy(
            spots, pall.at[pl.ds(z * nblk, nblk)], q_s.at[dz], q_r.at[dz], ((z + dz) % nrow, c), MESH)

    def up_copy(k):
        g = (last - k // ncol) * ncol + k % ncol
        return pltpu.make_async_remote_copy(group.at[g], ru.at[k], u_s.at[k], u_r.at[k], ((z + 1) % nrow, c), MESH)

    def down_copy(k):
        return pltpu.make_async_remote_copy(
            group.at[k], rd.at[k], d_s.at[k], d_r.at[k], ((z + nrow - 1) % nrow, c), MESH)

    def final_copy(j, i):
        s = block_of(j) * ncol + c
        return pltpu.make_async_remote_copy(
            group.at[z * ncol + i], got.at[s], f_s.at[i], f_r.at[s], (z, col_of(i)), MESH)

    def final_local(j):
        own = ncol - 1
        return pltpu.make_async_copy(group.at[z * ncol + own], got.at[block_of(j) * ncol + c], f_s.at[own])

    def load_cols(s, slot):
        return [pltpu.make_async_copy(
            integ.at[:, pl.ds(pl.multiple_of((s * tps + t) * TILE, TILE), TILE)],
            st.at[pl.ds((slot * tps + t) * depth, depth)], b_sem.at[slot * tps + t]) for t in range(tps)]

    def fetch(s, slot):
        for copy in load_cols(s, slot):
            copy.start()

    def arrive(s, slot):
        for copy in load_cols(s, slot):
            copy.wait()

    def load_amps(j):
        r = block_of(j)
        part_rows = arows // 2

        def begin(q):
            i, h = q // 2, q % 2
            e = (i + core) % 2
            at = pl.ds(h * part_rows, part_rows)
            own = (j + e) == 0

            @pl.when(own)
            def _():
                pltpu.make_async_copy(amps.at[at], ast.at[h], l_sem.at[h]).start()

            @pl.when(jnp.logical_not(own))
            def _():
                if h == 0:
                    amps_copy(j * 2 + e).wait_recv()
                pltpu.make_async_copy(aall.at[r * 2 + i, at], ast.at[h], l_sem.at[h]).start()

        begin(0)
        begin(1)
        for q in range(4):
            h = q % 2
            pltpu.make_async_copy(amps.at[pl.ds(0, part_rows)], ast.at[h], l_sem.at[h]).wait()

            @pl.loop(0, part_rows // 16)
            def _(n):
                at = pl.ds(pl.multiple_of(n * 16, 16), 16)
                to = pl.ds(pl.multiple_of(q * part_rows + n * 16, 16), 16)
                hi, lo = split(ast[h, at, :])
                ah[to, :] = hi
                al[to, :] = lo

            if q < 2:
                begin(q + 2)

    def dots(m, odd):
        bh, bl = bands[odd]
        acc = dot(ah[...], bh[m]) + dot(al[...], bh[m]) + dot(ah[...], bl[m])
        for t in range(tps):
            at = pl.ds(pl.multiple_of(((m * 2 + odd) * tps + t) * rows, rows), rows)
            part[at, :] = acc[:, t * TILE:(t + 1) * TILE]

    def split_cols(m, odd):
        bh, bl = bands[odd]
        for n in range(depth // TILE):
            at = pl.ds(n * TILE, TILE)
            for t in range(tps):
                cols = pl.ds(t * TILE, TILE)
                rows_at = pl.ds((odd * tps + t) * depth + n * TILE, TILE)
                hi, lo = split(st[rows_at, :] * mask_ref[n, (m * 2 + odd) * tps + t].astype(F32))
                bh[m, at, cols] = hi
                bl[m, at, cols] = lo

    for slot in range(2):
        fetch(slot, slot)
    barrier = pltpu.get_barrier_semaphore()
    for k in range(1, ncol):
        pl.semaphore_signal(barrier, 1, device_id=(z, peer(k)), device_id_type=MESH)
    for dz in range(1, nrow):
        pl.semaphore_signal(barrier, 1, device_id=((z + dz) % nrow, c), device_id_type=MESH)
    pl.semaphore_wait(barrier, ncol - 1 + nrow - 1)

    for dz in range(1, nrow):
        order_copy(dz).start()
        spots_copy(dz).start()
    for k in range(1, ncol):
        amps_copy(k).start()
    def to_scalar(src, r, n):
        at = pl.ds(pl.multiple_of(r * units, units), units)
        return pltpu.make_async_copy(src, idx.at[at], l_sem.at[2 + n])

    own_order = to_scalar(order, z, 0)
    own_order.start()

    arrive(0, 0)
    split_cols(0, 0)
    fetch(2, 0)
    load_amps(0)
    own_order.wait()
    for dz in range(1, nrow):
        order_copy(dz).wait()
        r = (z + nrow - dz) % nrow
        to_scalar(oall.at[pl.ds(pl.multiple_of(r * units, units), units)], r, dz).start()

    @pl.loop(0, half - 1)
    def _(m):
        arrive(m * 2 + 1, 1)
        split_cols(m, 1)
        dots(m, 0)
        fetch(m * 2 + 3, 1)
        arrive(m * 2 + 2, 0)
        split_cols(m + 1, 0)
        dots(m, 1)

        @pl.when(m < half - 2)
        def _():
            fetch(m * 2 + 4, 0)

    arrive(nsl - 1, 1)
    split_cols(half - 1, 1)
    dots(half - 1, 0)
    dots(half - 1, 1)
    for dz in range(1, nrow):
        to_scalar(order, 0, dz).wait()

    def places_remote(src, r, cc):
        return pltpu.make_async_remote_copy(
            src, gotp.at[r * ncol + c], p_s.at[r * ncol + cc], p_r.at[r * ncol + c], (z, cc), MESH)

    def places_local(src, r):
        return pltpu.make_async_copy(src, gotp.at[r * ncol + c], p_s.at[r * ncol + c])

    def send_places(n):
        r = n // ncol
        cc = n % ncol
        g = z * ncol + cc

        @pl.when(jnp.logical_and(cc == c, r == z))
        def _():
            places_local(spots.at[g], r).start()

        @pl.when(jnp.logical_and(cc == c, r != z))
        def _():
            places_local(pall.at[r * nblk + g], r).start()

        @pl.when(jnp.logical_and(cc != c, r == z))
        def _():
            places_remote(spots.at[g], r, cc).start()

        @pl.when(jnp.logical_and(cc != c, r != z))
        def _():
            places_remote(pall.at[r * nblk + g], r, cc).start()

    def wait_places():
        @pl.loop(0, nblk)
        def _(n):
            cc = n % ncol

            @pl.when(cc == c)
            def _():
                places_local(spots.at[0], n // ncol).wait()

            @pl.when(cc != c)
            def _():
                places_remote(spots.at[0], n // ncol, cc).wait_send()
                pltpu.make_async_copy(spots.at[0], gotp.at[n], p_r.at[n]).wait()

    lines = units // TILE

    def invert(n):
        lane = lax.broadcasted_iota(jnp.int32, (1, cap), 1)
        at = spot[n]
        high = jnp.right_shift(at, TILE.bit_length() - 1)
        here = lax.broadcasted_iota(jnp.int32, (lines, cap), 0) == high
        slot_high = (n * (cap // TILE) + lane // TILE).astype(F32)
        slot_low = (lane % TILE).astype(F32)
        left = jnp.concatenate(
            [jnp.where(here, slot_high, 0.0), jnp.where(here, slot_low, 0.0)], axis=0).astype(BF16)
        low_here = lax.broadcasted_iota(jnp.int32, (TILE, cap), 0) == jnp.bitwise_and(at, TILE - 1)
        right = jnp.where(low_here, 1.0, 0.0).astype(BF16)
        total[...] += lax.dot_general(left, right, (((1,), (1,)), ((), ())), preferred_element_type=F32)

    def publish():
        slot = (total[:lines, :] * TILE + total[lines:, :]).astype(jnp.int32)
        found[...] = jnp.clip(slot, 0, units - 1)
        copy = pltpu.make_async_copy(found, inv, l_sem.at[6])
        copy.start()
        copy.wait()

    def source_slot(j, cs):
        return ((cs // 4 + j // 2) % 2 * 2 + (cs // 2 % 2 + j % 2) % 2) * ncol + cs

    def landed(j, cs):
        n = source_slot(j, cs)

        @pl.when(cs != c)
        def _():
            pltpu.make_async_copy(group.at[0], got.at[n], f_r.at[n]).wait()

        return n

    early = nk * cap

    def gather_early():
        @pl.loop(0, nk)
        def _(t):
            n = landed(t // ncol, t % ncol)
            pltpu.make_async_copy(got.at[n], st.at[pl.ds(pl.multiple_of(n * cap, cap), cap)], l_sem.at[6]).start()

        pltpu.make_async_copy(pre.at[pl.ds(0, early)], st.at[pl.ds(0, early)], l_sem.at[6]).wait()

    def portion(k):
        @pl.loop(0, PORTION)
        def _(a):
            line = k * PORTION + a
            for u in range(TILE):
                part[pl.ds(line * TILE + u, 1), :] = st[pl.ds(inv[line, u], 1), :]

    def write_early():
        return pltpu.make_async_copy(part, pre, l_sem.at[7])

    def step(j, k):
        more = j < nrow - 1
        ku = k - (1 - low) * LAG
        kd = k - low * LAG
        d = last - ku // ncol

        @pl.when(jnp.logical_and(jnp.logical_and(z >= 1, ku >= 0), d >= z))
        def _():
            up_copy(ku).wait_recv()
            group[d * ncol + ku % ncol] += ru[ku]

            @pl.when(more)
            def _():
                pl.semaphore_signal(credit_u, 1, device_id=((z + nrow - 1) % nrow, c), device_id_type=MESH)

            @pl.when(d > z)
            def _():
                @pl.when(j > 0)
                def _():
                    pl.semaphore_wait(credit_u, 1)

                up_copy(ku).start()

        e = kd // ncol

        @pl.when(jnp.logical_and(jnp.logical_and(z < last, kd >= 0), e <= z))
        def _():
            down_copy(kd).wait_recv()
            group[kd] += rd[kd]

            @pl.when(more)
            def _():
                pl.semaphore_signal(credit_d, 1, device_id=((z + 1) % nrow, c), device_id_type=MESH)

            @pl.when(e < z)
            def _():
                @pl.when(j > 0)
                def _():
                    pl.semaphore_wait(credit_d, 1)

                down_copy(kd).start()

        kf = k - end * LAG + ncol
        i = kf % ncol

        @pl.when(kf // ncol == inner + 1)
        def _():
            @pl.when(i == ncol - 1)
            def _():
                final_local(j).start()

            @pl.when(i < ncol - 1)
            def _():
                final_copy(j, i).start()

    def wait_sent(g):
        d = g // ncol
        i = g % ncol

        @pl.when(d > z)
        def _():
            up_copy((last - d) * ncol + i).wait_send()

        @pl.when(d < z)
        def _():
            down_copy(g).wait_send()

        @pl.when(jnp.logical_and(d == z, i == ncol - 1))
        def _():
            final_local(0).wait()

        @pl.when(jnp.logical_and(d == z, i < ncol - 1))
        def _():
            final_copy(0, i).wait_send()

    gap = nk // LAG
    per = (nk - LAG) // half
    nportion = units // TILE // PORTION

    @pl.loop(0, nrow)
    def _(j):
        base = block_of(j) * units

        def order_piece(n):
            q = n // ncol
            p = n % ncol
            d = low * (last - q) + (1 - low) * q
            g = d * ncol + p
            start = base + (d * ncol + col_of(p)) * cap

            @pl.when(j > 0)
            def _():
                wait_sent(g)

            @pl.loop(0, cap // UNROLL)
            def _(i):
                first = start + i * UNROLL
                for u in range(UNROLL):
                    group[g, pl.ds(i * UNROLL + u, 1), :] = part[pl.ds(idx[first + u], 1), :]

            @pl.when(jnp.logical_and(z == 0, d > 0))
            def _():
                @pl.when(j > 0)
                def _():
                    pl.semaphore_wait(credit_u, 1)

                up_copy((last - d) * ncol + p).start()

            @pl.when(jnp.logical_and(z == last, d < last))
            def _():
                @pl.when(j > 0)
                def _():
                    pl.semaphore_wait(credit_d, 1)

                down_copy(g).start()

            @pl.when(jnp.logical_and(jnp.logical_and(end == 0, n < LAG * gap), n % gap == gap - 1))
            def _():
                step(j, n // gap)

        pl.loop(0, nk)(order_piece)

        @pl.when(jnp.logical_and(j > 0, end == 1))
        def _():
            @pl.loop(0, nk)
            def _(k):
                step(j - 1, k)

        pl.loop(nk, nblk)(order_piece)

        @pl.when(j == 0)
        def _():
            for dz in range(1, nrow):
                spots_copy(dz).wait()
            pl.loop(0, nblk)(send_places)

        @pl.when(j == 1)
        def _():
            wait_places()
            copy = pltpu.make_async_copy(gotp, spot, l_sem.at[6])
            copy.start()
            copy.wait()
            total[...] = jnp.zeros_like(total)

        @pl.when(j < nrow - 1)
        def _():
            load_amps(j + 1)

        @pl.when(j == nrow - 1)
        def _():
            gather_early()

        @pl.loop(0, half)
        def _(m):
            @pl.when(j < nrow - 1)
            def _():
                dots(m, 0)
                dots(m, 1)

            @pl.loop(0, per)
            def _(i):
                n = m * per + i

                @pl.when(jnp.logical_or(end == 0, j == nrow - 1))
                def _():
                    step(j, n + LAG)

                @pl.when(jnp.logical_and(j == 1, n < nblk // 2))
                def _():
                    invert(n * 2)
                    invert(n * 2 + 1)

                @pl.when(jnp.logical_and(j == 1, n == nblk // 2))
                def _():
                    publish()

                @pl.when(jnp.logical_and(j == nrow - 1, n < nportion))
                def _():
                    portion(n)

                @pl.when(jnp.logical_and(j == nrow - 1, n == nportion))
                def _():
                    write_early().start()

    @pl.loop(0, nblk)
    def _(g):
        wait_sent(g)

    for k in range(1, ncol):
        amps_copy(k).wait_send()

    @pl.loop(0, ncol)
    def _(cs):
        landed(nrow - 1, cs)

    write_early().wait()


def exchange(amps, integrals, mask, order, spots, nrow, ncol):
    arows, depth = amps.shape
    cols = integrals.shape[1]
    nblk = nrow * ncol
    rows = arows * ncol // nrow
    units = rows * cols // TILE
    cap = units // nblk
    nsl = cols // SLICE
    nk = (nrow - 1) * ncol
    any_spec = pl.BlockSpec(memory_space=pl.ANY)
    dma = pltpu.SemaphoreType.DMA
    got, gotp, pre, _, _, _ = pl.pallas_call(
        functools.partial(exchange_kernel, nrow, ncol),
        out_shape=[
            jax.ShapeDtypeStruct((nblk, cap, TILE), F32),
            jax.ShapeDtypeStruct((nblk, 1, cap), jnp.int32),
            jax.ShapeDtypeStruct((units, TILE), F32),
            jax.ShapeDtypeStruct((ncol, arows, depth), F32),
            jax.ShapeDtypeStruct((nrow * units,), jnp.int32),
            jax.ShapeDtypeStruct((nrow * nblk, 1, cap), jnp.int32),
        ],
        in_specs=[pl.BlockSpec(memory_space=pltpu.SMEM)] + [any_spec] * 4,
        out_specs=[any_spec] * 6,
        scratch_shapes=[
            pltpu.VMEM((2 * SLICE // TILE * depth, TILE), F32),
            pltpu.VMEM((2, arows // 2, depth), F32),
            pltpu.VMEM((rows, depth), BF16),
            pltpu.VMEM((rows, depth), BF16),
            pltpu.VMEM((nsl // 2, depth, SLICE), BF16),
            pltpu.VMEM((nsl // 2, depth, SLICE), BF16),
            pltpu.VMEM((nsl // 2, depth, SLICE), BF16),
            pltpu.VMEM((nsl // 2, depth, SLICE), BF16),
            pltpu.VMEM((units, TILE), F32),
            pltpu.VMEM((nblk, cap, TILE), F32),
            pltpu.VMEM((nk, cap, TILE), F32),
            pltpu.VMEM((nk, cap, TILE), F32),
            pltpu.SMEM((nrow * units,), jnp.int32),
            pltpu.VMEM((nblk, 1, cap), jnp.int32),
            pltpu.VMEM((2 * units // TILE, TILE), F32),
            pltpu.VMEM((units // TILE, TILE), jnp.int32),
            pltpu.SMEM((units // TILE, TILE), jnp.int32),
            dma((ncol,)), dma((ncol,)), dma((nrow,)), dma((nrow,)), dma((nrow,)), dma((nrow,)),
            dma((nblk,)), dma((nblk,)),
            dma((nk,)), dma((nk,)), dma((nk,)), dma((nk,)), dma((ncol,)), dma((nblk,)),
            dma((2 * SLICE // TILE,)), dma((8,)),
            pltpu.SemaphoreType.REGULAR, pltpu.SemaphoreType.REGULAR,
        ],
        compiler_params=pltpu.CompilerParams(
            collective_id=0, has_side_effects=True, vmem_limit_bytes=67043328),
        name="exchange",
    )(mask, amps, integrals, order, spots)
    return got, gotp, pre


def place_kernel(nrow, ncol, tpb, spot_ref, mask_ref, got, pre, den_ref, cyc_ref, upd_ref, term_ref,
                 moved, late, c_hi, c_lo, sems):
    rows = den_ref.shape[0]
    cap = got.shape[1]
    k = pl.program_id(0)

    @pl.when(k == 0)
    def _():
        copies = [pltpu.make_async_copy(pre, moved, sems.at[ncol])]
        slots = []
        for cs in range(ncol):
            j = nrow - 1
            n = ((cs // 4 + j // 2) % 2 * 2 + (cs // 2 % 2 + j % 2) % 2) * ncol + cs
            slots.append(n)
            copies.append(pltpu.make_async_copy(got.at[n], late.at[cs], sems.at[cs]))
        for copy in copies:
            copy.start()
        for copy in copies:
            copy.wait()
        for cs in range(ncol):
            @pl.loop(0, cap // UNROLL)
            def _(i):
                first = slots[cs] * cap + i * UNROLL
                for u in range(UNROLL):
                    moved[pl.ds(spot_ref[first + u], 1), :] = late[cs, pl.ds(i * UNROLL + u, 1), :]

    for u in range(tpb):
        for s in range(tpb):
            at = (pl.ds(u * TILE, TILE), pl.ds(s * TILE, TILE))
            hi, lo = split(cyc_ref[at] * mask_ref[k * tpb + u, s].astype(F32))
            c_hi[at] = hi
            c_lo[at] = lo
    tiles = [moved[pl.ds(pl.multiple_of((k * tpb + t) * rows, rows), rows), :] for t in range(tpb)]
    upd = jnp.concatenate(tiles, axis=1) / den_ref[...]
    upd_ref[...] = upd
    hi, lo = split(upd)
    term_ref[...] = dot(hi, c_hi[...]) + dot(lo, c_hi[...]) + dot(hi, c_lo[...])


def place(got, gotp, pre, nrow, ncol, denominators, cycle_tiles, cycle_mask):
    rows, cols = denominators.shape
    rb = cycle_tiles.shape[1]
    units = rows * cols // TILE
    out = jax.ShapeDtypeStruct((rows, cols), F32)
    block = pl.BlockSpec((rows, rb), lambda i, s, m: (0, i))
    return pl.pallas_call(
        functools.partial(place_kernel, nrow, ncol, rb // TILE),
        out_shape=[out, out],
        grid_spec=pltpu.PrefetchScalarGridSpec(
            num_scalar_prefetch=2,
            grid=(cols // rb,),
            in_specs=[
                pl.BlockSpec(memory_space=pl.ANY),
                pl.BlockSpec(memory_space=pl.ANY),
                block,
                pl.BlockSpec((rb, rb), lambda i, s, m: (i, 0)),
            ],
            out_specs=[block, block],
            scratch_shapes=[
                pltpu.VMEM((units, TILE), F32),
                pltpu.VMEM((ncol,) + got.shape[1:], F32),
                pltpu.VMEM((rb, rb), BF16),
                pltpu.VMEM((rb, rb), BF16),
                pltpu.SemaphoreType.DMA((ncol + 1,)),
            ],
        ),
        compiler_params=pltpu.CompilerParams(vmem_limit_bytes=62 * 2**20),
        name="place",
    )(gotp.reshape(-1), cycle_mask, got, pre, denominators, cycle_tiles)


def sorted_keys(destination, nrow, ncol):
    rows, tiles = destination.shape
    vt = tiles * ncol
    units = rows * tiles
    flat = destination.T.reshape(-1)
    out_row = flat // vt
    out_tile = flat % vt
    owner = out_row // rows * ncol + out_tile // tiles
    spot = out_tile % tiles * rows + out_row % rows
    key = (owner * units + spot) * units + lax.iota(jnp.int32, units)
    ndev = nrow * ncol
    key = lax.sort(key, is_stable=False)
    return key % units, (key // units % units).reshape(ndev, 1, units // ndev)


def direct(amplitudes, integrals, integral_mask, denominators, cycle_tiles, cycle_mask, destination):
    nrow = lax.axis_size("row")
    ncol = lax.axis_size("col")
    order, spots = sorted_keys(destination, nrow, ncol)
    got, gotp, pre = exchange(amplitudes, integrals, integral_mask, order, spots, nrow, ncol)
    return tuple(place(got, gotp, pre, nrow, ncol, denominators, cycle_tiles, cycle_mask))


def solution(mesh):
    step = direct if (mesh.shape["row"], mesh.shape["col"]) == (4, 8) else body
    return jax.shard_map(
        step,
        mesh=mesh,
        in_specs=(
            P("col", "row"),
            P("row", "col"),
            P("row", "col"),
            P("row", "col"),
            P("col", None),
            P("col", None),
            P("row", "col"),
        ),
        out_specs=(P("row", "col"), P("row", "col")),
        check_vma=False,
    )
```

```python
import functools
import jax
import jax.numpy as jnp
from jax import lax
from jax.experimental import pallas as pl
from jax.experimental.pallas import tpu as pltpu
from jax.sharding import PartitionSpec as P

TILE = 128
F32 = jnp.float32
BF16 = jnp.bfloat16
CHUNKS = 4


def split(x):
    hi = x.astype(BF16)
    return hi, (x - hi.astype(F32)).astype(BF16)


def dot(a, b):
    return jnp.dot(a, b, preferred_element_type=F32)


def product_kernel(nblk, first_tile, tpb, off_ref, mask_ref, a_ref, b_ref, *rest):
    outs, (a_hi, a_lo, b_hi, b_lo) = rest[:-4], rest[-4:]
    rows, depth = a_ref.shape
    blk = rows // nblk
    step = pl.program_id(0)

    @pl.when(step == 0)
    def _():
        for j in range(nblk):
            src = pl.multiple_of(off_ref[j] * blk, blk)
            hi, lo = split(a_ref[pl.ds(src, blk), :])
            a_hi[pl.ds(j * blk, blk), :] = hi
            a_lo[pl.ds(j * blk, blk), :] = lo

    @pl.loop(0, depth // TILE)
    def _(c):
        at = pl.ds(pl.multiple_of(c * TILE, TILE), TILE)
        for t in range(tpb):
            cols = pl.ds(t * TILE, TILE)
            m = mask_ref[c, first_tile + step * tpb + t].astype(F32)
            hi, lo = split(b_ref[at, cols] * m)
            b_hi[at, cols] = hi
            b_lo[at, cols] = lo

    big = rows // 2
    piece = rows // len(outs)
    per = big // piece if big >= piece else 1
    for h in range(2):
        at = pl.ds(h * big, big)
        acc = dot(a_hi[at, :], b_hi[...]) + dot(a_lo[at, :], b_hi[...]) + dot(a_hi[at, :], b_lo[...])
        for t in range(tpb):
            col = acc[:, t * TILE:(t + 1) * TILE]
            if len(outs) == 1:
                outs[0][t, at, :] = col
            else:
                for q in range(per):
                    outs[h * per + q][t, :, :] = col[q * piece:(q + 1) * piece]


def product(amps, integrals, mask, offsets, chunk, nblk, npieces):
    rows, depth = amps.shape
    cols = integrals.shape[1]
    width = cols // CHUNKS
    tpb = min(4, width // TILE)
    bn = tpb * TILE
    steps = width // bn
    piece = rows // npieces
    out = jax.ShapeDtypeStruct((width // TILE, piece, TILE), F32)
    return pl.pallas_call(
        functools.partial(product_kernel, nblk, chunk * (width // TILE), tpb),
        out_shape=[out] * npieces,
        grid_spec=pltpu.PrefetchScalarGridSpec(
            num_scalar_prefetch=2,
            grid=(steps,),
            in_specs=[
                pl.BlockSpec((rows, depth), lambda i, o, m: (0, 0), pipeline_mode=pl.Buffered(1)),
                pl.BlockSpec((depth, bn), lambda i, o, m: (0, chunk * steps + i)),
            ],
            out_specs=[pl.BlockSpec((tpb, piece, TILE), lambda i, o, m: (i, 0, 0))] * npieces,
            scratch_shapes=[
                pltpu.VMEM((rows, depth), BF16),
                pltpu.VMEM((rows, depth), BF16),
                pltpu.VMEM((depth, bn), BF16),
                pltpu.VMEM((depth, bn), BF16),
            ],
        ),
        cost_estimate=pl.CostEstimate(
            flops=6 * rows * depth * width,
            bytes_accessed=4 * (rows * depth + depth * width + rows * width),
            transcendentals=0,
        ),
        compiler_params=pltpu.CompilerParams(vmem_limit_bytes=56 * 2**20),
        name="product",
    )(offsets, mask, amps, integrals)


def gather_kernel(idx_ref, x_ref, o_ref):
    n = o_ref.shape[0]
    base = pl.program_id(0) * n

    @pl.loop(0, n // 16)
    def _(i):
        for u in range(16):
            k = i * 16 + u
            o_ref[pl.ds(k, 1), :] = x_ref[pl.ds(idx_ref[base + k], 1), :]


def gather_units(units, idx):
    n = units.shape[0]
    bn = min(1024, n)
    return pl.pallas_call(
        gather_kernel,
        out_shape=jax.ShapeDtypeStruct(units.shape, F32),
        grid_spec=pltpu.PrefetchScalarGridSpec(
            num_scalar_prefetch=1,
            grid=(n // bn,),
            in_specs=[pl.BlockSpec(units.shape, lambda i, s: (0, 0), pipeline_mode=pl.Buffered(1))],
            out_specs=pl.BlockSpec((bn, TILE), lambda i, s: (i, 0)),
        ),
        compiler_params=pltpu.CompilerParams(vmem_limit_bytes=24 * 2**20),
        name="gather_units",
    )(idx, units)


def finish_kernel(tiles, tpb, idx_ref, mask_ref, got_ref, den_ref, cyc_ref, upd_ref, term_ref, moved, c_hi, c_lo):
    rows = den_ref.shape[0]
    k = pl.program_id(0)

    @pl.loop(0, rows // 8)
    def _(i):
        for u in range(8):
            r = i * 8 + u
            for t in range(tpb):
                q = idx_ref[r * tiles + k * tpb + t]
                moved[t, pl.ds(r, 1), :] = got_ref[pl.ds(q, 1), :]

    for u in range(tpb):
        for s in range(tpb):
            at = (pl.ds(u * TILE, TILE), pl.ds(s * TILE, TILE))
            hi, lo = split(cyc_ref[at] * mask_ref[k * tpb + u, s].astype(F32))
            c_hi[at] = hi
            c_lo[at] = lo
    upd = jnp.concatenate([moved[t] for t in range(tpb)], axis=1) / den_ref[...]
    upd_ref[...] = upd
    hi, lo = split(upd)
    term_ref[...] = dot(hi, c_hi[...]) + dot(lo, c_hi[...]) + dot(hi, c_lo[...])


def finish(got, inv, denominators, cycle_tiles, cycle_mask):
    rows, cols = denominators.shape
    rb = cycle_tiles.shape[1]
    out = jax.ShapeDtypeStruct((rows, cols), F32)
    block = pl.BlockSpec((rows, rb), lambda i, s, m: (0, i))
    return pl.pallas_call(
        functools.partial(finish_kernel, cols // TILE, rb // TILE),
        out_shape=[out, out],
        grid_spec=pltpu.PrefetchScalarGridSpec(
            num_scalar_prefetch=2,
            grid=(cols // rb,),
            in_specs=[
                pl.BlockSpec(got.shape, lambda i, s, m: (0, 0), pipeline_mode=pl.Buffered(1)),
                block,
                pl.BlockSpec((rb, rb), lambda i, s, m: (i, 0)),
            ],
            out_specs=[block, block],
            scratch_shapes=[
                pltpu.VMEM((rb // TILE, rows, TILE), F32),
                pltpu.VMEM((rb, rb), BF16),
                pltpu.VMEM((rb, rb), BF16),
            ],
        ),
        compiler_params=pltpu.CompilerParams(vmem_limit_bytes=40 * 2**20),
        name="finish",
    )(inv, cycle_mask, got, denominators, cycle_tiles)


def routes(destination, nrow, ncol):
    local_rows, local_tiles = destination.shape
    vt = local_tiles * ncol
    units = local_rows * local_tiles
    half = local_rows // 2
    tc = local_tiles // CHUNKS
    flat = destination.reshape(2, half, CHUNKS, tc).transpose(2, 0, 3, 1).reshape(-1)
    out_row = flat // vt
    out_tile = flat % vt
    owner = out_row // local_rows * ncol + out_tile // local_tiles
    place = out_row % local_rows * local_tiles + out_tile % local_tiles
    iota = lax.iota(jnp.int32, units)
    key, order = lax.sort((owner * units + place, iota), num_keys=1, is_stable=False)
    ndev = nrow * ncol
    places = (key % units).astype(F32).reshape(ndev, units // ndev)
    got_place = lax.all_to_all(places, ("row", "col"), split_axis=0, concat_axis=0, tiled=True)
    _, inv = lax.sort((got_place.reshape(-1).astype(jnp.int32), iota), num_keys=1, is_stable=False)
    return order, inv


def body(amplitudes, integrals, integral_mask, denominators, cycle_tiles, cycle_mask, destination):
    nrow = lax.axis_size("row")
    ncol = lax.axis_size("col")
    me = lax.axis_index("row")
    amps = lax.all_gather(amplitudes, "col", axis=0, tiled=True)
    order, inv = routes(destination, nrow, ncol)
    local_rows = destination.shape[0]
    half = local_rows // 2
    pieces = []
    if nrow == 4:
        up = [(i, (i + 1) % nrow) for i in range(nrow)]
        down = [(i, (i - 1) % nrow) for i in range(nrow)]
        offsets = jnp.stack([(me + d) % nrow for d in (2, 1, 3, 0)]).astype(jnp.int32)
        sent, landed = [], []
        for c in range(CHUNKS):
            if c >= 2:
                after = sent[c - 2] + (landed[c - 3] if c >= 3 else [])
                offsets = lax.optimization_barrier([offsets] + after)[0]
            far_a, far_b, up_a, up_b, dn_a, dn_b, own_a, own_b = product(
                amps, integrals, integral_mask, offsets, c, nrow, 2 * nrow)
            in_a = lax.ppermute(far_a, "row", up)
            in_b = lax.ppermute(far_b, "row", down)
            direct_b = lax.ppermute(up_b, "row", up)
            direct_a = lax.ppermute(dn_a, "row", down)
            next_a, next_b = up_a + in_a, dn_b + in_b
            sum_a = lax.ppermute(next_a, "row", up)
            sum_b = lax.ppermute(next_b, "row", down)
            sent.append([next_a, next_b, direct_a, direct_b])
            landed.append([sum_a, sum_b])
            pieces.append(own_a + direct_a + sum_a)
            pieces.append(own_b + direct_b + sum_b)
    else:
        offsets = lax.iota(jnp.int32, nrow)
        for c in range(CHUNKS):
            (part,) = product(amps, integrals, integral_mask, offsets, c, nrow, 1)
            summed = lax.psum_scatter(part, "row", scatter_dimension=1, tiled=True)
            pieces.append(summed[:, :half])
            pieces.append(summed[:, half:])
    units = jnp.concatenate([p.reshape(-1, TILE) for p in pieces], axis=0)
    sending = gather_units(units, order)
    ndev = nrow * ncol
    got = lax.all_to_all(sending.reshape(ndev, -1, TILE), ("row", "col"), split_axis=0, concat_axis=0, tiled=True)
    return tuple(finish(got.reshape(-1, TILE), inv, denominators, cycle_tiles, cycle_mask))


MESH = pl.DeviceIdType.MESH
SLICE = 512
UNROLL = 16
LAG = 4
PORTION = 4
PAIR = 2


def exchange_kernel(nrow, ncol, mask_ref, amps, integ, order, spots, got, gotp, pre, aall, oall, pall,
                    st, ast, ah, al, bh0, bl0, bh1, bl1, part, group, ru, rd, idx, spot, total, found, inv,
                    a_s, a_r, o_s, o_r, q_s, q_r, p_s, p_r, u_s, u_r, d_s, d_r, f_s, f_r, b_sem, l_sem, credit_u, credit_d):
    z = lax.axis_index("row")
    c = lax.axis_index("col")
    last = nrow - 1
    arows, depth = amps.shape
    nblk, cap = got.shape[0], got.shape[1]
    units = nblk * cap
    half, _, width = bh0.shape
    nsl = half * 2
    bands = (bh0, bl0), (bh1, bl1)
    tps = width // TILE
    rows = ah.shape[0]
    nk = last * ncol
    low = 1 - z // 2
    inner = z * (last - z)
    end = 1 - (inner + 1) // 2
    core = c % 2
    cx = c // 2 % 2
    cy = c // 4

    def peer(k):
        px = (cx + k // 2 % 2) % 2
        py = (cy + k // 4) % 2
        return (py * 2 + px) * 2 + (core + k % 2) % 2

    def col_of(i):
        return peer(ncol - 1 - i)

    def block_of(j):
        return (cy + j // 2) % 2 * 2 + (cx + j % 2) % 2

    def amps_copy(k):
        return pltpu.make_async_remote_copy(amps, aall.at[c], a_s.at[k], a_r.at[k], (z, peer(k)), MESH)

    def order_copy(dz):
        at = pl.ds(pl.multiple_of(z * units, units), units)
        return pltpu.make_async_remote_copy(order, oall.at[at], o_s.at[dz], o_r.at[dz], ((z + dz) % nrow, c), MESH)

    def spots_copy(dz):
        return pltpu.make_async_remote_copy(
            spots, pall.at[pl.ds(z * nblk, nblk)], q_s.at[dz], q_r.at[dz], ((z + dz) % nrow, c), MESH)

    def up_copy(k):
        g = (last - k // ncol) * ncol + k % ncol
        return pltpu.make_async_remote_copy(group.at[g], ru.at[k], u_s.at[k], u_r.at[k], ((z + 1) % nrow, c), MESH)

    def down_copy(k):
        return pltpu.make_async_remote_copy(
            group.at[k], rd.at[k], d_s.at[k], d_r.at[k], ((z + nrow - 1) % nrow, c), MESH)

    def final_copy(j, i):
        s = block_of(j) * ncol + c
        return pltpu.make_async_remote_copy(
            group.at[z * ncol + i], got.at[s], f_s.at[i], f_r.at[s], (z, col_of(i)), MESH)

    def final_local(j):
        own = ncol - 1
        return pltpu.make_async_copy(group.at[z * ncol + own], got.at[block_of(j) * ncol + c], f_s.at[own])

    def load_cols(s, slot):
        return [pltpu.make_async_copy(
            integ.at[:, pl.ds(pl.multiple_of((s * tps + t) * TILE, TILE), TILE)],
            st.at[pl.ds((slot * tps + t) * depth, depth)], b_sem.at[slot * tps + t]) for t in range(tps)]

    def fetch(s, slot):
        for copy in load_cols(s, slot):
            copy.start()

    def arrive(s, slot):
        for copy in load_cols(s, slot):
            copy.wait()

    def load_amps(j):
        r = block_of(j)
        part_rows = arows // 2

        def begin(q):
            i, h = q // 2, q % 2
            e = (i + core) % 2
            at = pl.ds(h * part_rows, part_rows)
            own = (j + e) == 0

            @pl.when(own)
            def _():
                pltpu.make_async_copy(amps.at[at], ast.at[h], l_sem.at[h]).start()

            @pl.when(jnp.logical_not(own))
            def _():
                if h == 0:
                    amps_copy(j * 2 + e).wait_recv()
                pltpu.make_async_copy(aall.at[r * 2 + i, at], ast.at[h], l_sem.at[h]).start()

        begin(0)
        begin(1)
        for q in range(4):
            h = q % 2
            pltpu.make_async_copy(amps.at[pl.ds(0, part_rows)], ast.at[h], l_sem.at[h]).wait()

            @pl.loop(0, part_rows // 16)
            def _(n):
                at = pl.ds(pl.multiple_of(n * 16, 16), 16)
                to = pl.ds(pl.multiple_of(q * part_rows + n * 16, 16), 16)
                hi, lo = split(ast[h, at, :])
                ah[to, :] = hi
                al[to, :] = lo

            if q < 2:
                begin(q + 2)

    def dots(m, odd):
        bh, bl = bands[odd]
        acc = dot(ah[...], bh[m]) + dot(al[...], bh[m]) + dot(ah[...], bl[m])
        for t in range(tps):
            at = pl.ds(pl.multiple_of(((m * 2 + odd) * tps + t) * rows, rows), rows)
            part[at, :] = acc[:, t * TILE:(t + 1) * TILE]

    def split_cols(m, odd):
        bh, bl = bands[odd]
        for n in range(depth // TILE):
            at = pl.ds(n * TILE, TILE)
            for t in range(tps):
                cols = pl.ds(t * TILE, TILE)
                rows_at = pl.ds((odd * tps + t) * depth + n * TILE, TILE)
                hi, lo = split(st[rows_at, :] * mask_ref[n, (m * 2 + odd) * tps + t].astype(F32))
                bh[m, at, cols] = hi
                bl[m, at, cols] = lo

    for slot in range(2):
        fetch(slot, slot)
    barrier = pltpu.get_barrier_semaphore()
    for k in range(1, ncol):
        pl.semaphore_signal(barrier, 1, device_id=(z, peer(k)), device_id_type=MESH)
    for dz in range(1, nrow):
        pl.semaphore_signal(barrier, 1, device_id=((z + dz) % nrow, c), device_id_type=MESH)
    pl.semaphore_wait(barrier, ncol - 1 + nrow - 1)

    for dz in range(1, nrow):
        order_copy(dz).start()
        spots_copy(dz).start()
    for k in range(1, ncol):
        amps_copy(k).start()
    def to_scalar(src, r, n):
        at = pl.ds(pl.multiple_of(r * units, units), units)
        return pltpu.make_async_copy(src, idx.at[at], l_sem.at[2 + n])

    own_order = to_scalar(order, z, 0)
    own_order.start()

    arrive(0, 0)
    split_cols(0, 0)
    fetch(2, 0)
    load_amps(0)
    own_order.wait()
    for dz in range(1, nrow):
        order_copy(dz).wait()
        r = (z + nrow - dz) % nrow
        to_scalar(oall.at[pl.ds(pl.multiple_of(r * units, units), units)], r, dz).start()

    @pl.loop(0, half - 1)
    def _(m):
        arrive(m * 2 + 1, 1)
        split_cols(m, 1)
        dots(m, 0)
        fetch(m * 2 + 3, 1)
        arrive(m * 2 + 2, 0)
        split_cols(m + 1, 0)
        dots(m, 1)

        @pl.when(m < half - 2)
        def _():
            fetch(m * 2 + 4, 0)

    arrive(nsl - 1, 1)
    split_cols(half - 1, 1)
    dots(half - 1, 0)
    dots(half - 1, 1)
    for dz in range(1, nrow):
        to_scalar(order, 0, dz).wait()

    def places_remote(src, r, cc):
        return pltpu.make_async_remote_copy(
            src, gotp.at[r * ncol + c], p_s.at[r * ncol + cc], p_r.at[r * ncol + c], (z, cc), MESH)

    def places_local(src, r):
        return pltpu.make_async_copy(src, gotp.at[r * ncol + c], p_s.at[r * ncol + c])

    def send_places(n):
        r = n // ncol
        cc = n % ncol
        g = z * ncol + cc

        @pl.when(jnp.logical_and(cc == c, r == z))
        def _():
            places_local(spots.at[g], r).start()

        @pl.when(jnp.logical_and(cc == c, r != z))
        def _():
            places_local(pall.at[r * nblk + g], r).start()

        @pl.when(jnp.logical_and(cc != c, r == z))
        def _():
            places_remote(spots.at[g], r, cc).start()

        @pl.when(jnp.logical_and(cc != c, r != z))
        def _():
            places_remote(pall.at[r * nblk + g], r, cc).start()

    def wait_places():
        @pl.loop(0, nblk)
        def _(n):
            cc = n % ncol

            @pl.when(cc == c)
            def _():
                places_local(spots.at[0], n // ncol).wait()

            @pl.when(cc != c)
            def _():
                places_remote(spots.at[0], n // ncol, cc).wait_send()
                pltpu.make_async_copy(spots.at[0], gotp.at[n], p_r.at[n]).wait()

    lines = units // TILE

    def invert(n):
        lane = lax.broadcasted_iota(jnp.int32, (1, cap), 1)
        at = spot[n]
        high = jnp.right_shift(at, TILE.bit_length() - 1)
        here = lax.broadcasted_iota(jnp.int32, (lines, cap), 0) == high
        slot_high = (n * (cap // TILE) + lane // TILE).astype(F32)
        slot_low = (lane % TILE).astype(F32)
        left = jnp.concatenate(
            [jnp.where(here, slot_high, 0.0), jnp.where(here, slot_low, 0.0)], axis=0).astype(BF16)
        low_here = lax.broadcasted_iota(jnp.int32, (TILE, cap), 0) == jnp.bitwise_and(at, TILE - 1)
        right = jnp.where(low_here, 1.0, 0.0).astype(BF16)
        total[...] += lax.dot_general(left, right, (((1,), (1,)), ((), ())), preferred_element_type=F32)

    def publish():
        slot = (total[:lines, :] * TILE + total[lines:, :]).astype(jnp.int32)
        found[...] = jnp.clip(slot, 0, units - 1)
        copy = pltpu.make_async_copy(found, inv, l_sem.at[6])
        copy.start()
        copy.wait()

    def source_slot(j, cs):
        return ((cs // 4 + j // 2) % 2 * 2 + (cs // 2 % 2 + j % 2) % 2) * ncol + cs

    def landed(j, cs):
        n = source_slot(j, cs)

        @pl.when(cs != c)
        def _():
            pltpu.make_async_copy(group.at[0], got.at[n], f_r.at[n]).wait()

        return n

    early = nk * cap

    def gather_early():
        @pl.loop(0, nk)
        def _(t):
            n = landed(t // ncol, t % ncol)
            pltpu.make_async_copy(got.at[n], st.at[pl.ds(pl.multiple_of(n * cap, cap), cap)], l_sem.at[6]).start()

        pltpu.make_async_copy(pre.at[pl.ds(0, early)], st.at[pl.ds(0, early)], l_sem.at[6]).wait()

    def portion(k):
        @pl.loop(0, PORTION)
        def _(a):
            line = k * PORTION + a
            for u in range(TILE):
                part[pl.ds(line * TILE + u, 1), :] = st[pl.ds(inv[line, u], 1), :]

    def write_early():
        return pltpu.make_async_copy(part, pre, l_sem.at[7])

    def step(j, k):
        more = j < nrow - 1
        ku = k - (1 - low) * LAG
        kd = k - low * LAG
        d = last - ku // ncol

        @pl.when(jnp.logical_and(jnp.logical_and(z >= 1, ku >= 0), d >= z))
        def _():
            up_copy(ku).wait_recv()
            group[d * ncol + ku % ncol] += ru[ku]

            @pl.when(more)
            def _():
                pl.semaphore_signal(credit_u, 1, device_id=((z + nrow - 1) % nrow, c), device_id_type=MESH)

            @pl.when(d > z)
            def _():
                @pl.when(j > 0)
                def _():
                    pl.semaphore_wait(credit_u, 1)

                up_copy(ku).start()

        e = kd // ncol

        @pl.when(jnp.logical_and(jnp.logical_and(z < last, kd >= 0), e <= z))
        def _():
            down_copy(kd).wait_recv()
            group[kd] += rd[kd]

            @pl.when(more)
            def _():
                pl.semaphore_signal(credit_d, 1, device_id=((z + 1) % nrow, c), device_id_type=MESH)

            @pl.when(e < z)
            def _():
                @pl.when(j > 0)
                def _():
                    pl.semaphore_wait(credit_d, 1)

                down_copy(kd).start()

        kf = k - end * LAG + ncol
        i = kf % ncol

        @pl.when(kf // ncol == inner + 1)
        def _():
            @pl.when(i == ncol - 1)
            def _():
                final_local(j).start()

            @pl.when(i < ncol - 1)
            def _():
                final_copy(j, i).start()

    def wait_sent(g):
        d = g // ncol
        i = g % ncol

        @pl.when(d > z)
        def _():
            up_copy((last - d) * ncol + i).wait_send()

        @pl.when(d < z)
        def _():
            down_copy(g).wait_send()

        @pl.when(jnp.logical_and(d == z, i == ncol - 1))
        def _():
            final_local(0).wait()

        @pl.when(jnp.logical_and(d == z, i < ncol - 1))
        def _():
            final_copy(0, i).wait_send()

    gap = nk // LAG
    per = (nk - LAG) // half
    nportion = units // TILE // PORTION

    @pl.loop(0, nrow)
    def _(j):
        base = block_of(j) * units

        def order_piece(n):
            q = n // ncol
            p = n % ncol
            d = low * (last - q) + (1 - low) * q
            g = d * ncol + p
            start = base + (d * ncol + col_of(p)) * cap

            @pl.when(j > 0)
            def _():
                wait_sent(g)

            @pl.loop(0, cap // UNROLL)
            def _(i):
                first = start + i * UNROLL
                for u in range(UNROLL):
                    group[g, pl.ds(i * UNROLL + u, 1), :] = part[pl.ds(idx[first + u], 1), :]

            @pl.when(jnp.logical_and(z == 0, d > 0))
            def _():
                @pl.when(j > 0)
                def _():
                    pl.semaphore_wait(credit_u, 1)

                up_copy((last - d) * ncol + p).start()

            @pl.when(jnp.logical_and(z == last, d < last))
            def _():
                @pl.when(j > 0)
                def _():
                    pl.semaphore_wait(credit_d, 1)

                down_copy(g).start()

            @pl.when(jnp.logical_and(jnp.logical_and(end == 0, n < LAG * gap), n % gap == gap - 1))
            def _():
                step(j, n // gap)

        pl.loop(0, nk)(order_piece)

        @pl.when(jnp.logical_and(j > 0, end == 1))
        def _():
            @pl.loop(0, nk)
            def _(k):
                step(j - 1, k)

        pl.loop(nk, nblk)(order_piece)

        @pl.when(j == 0)
        def _():
            for dz in range(1, nrow):
                spots_copy(dz).wait()
            pl.loop(0, nblk)(send_places)

        @pl.when(j == 1)
        def _():
            wait_places()
            copy = pltpu.make_async_copy(gotp, spot, l_sem.at[6])
            copy.start()
            copy.wait()
            total[...] = jnp.zeros_like(total)

        @pl.when(j < nrow - 1)
        def _():
            load_amps(j + 1)

        @pl.when(j == nrow - 1)
        def _():
            gather_early()

        @pl.loop(0, half)
        def _(m):
            @pl.when(j < nrow - 1)
            def _():
                dots(m, 0)
                dots(m, 1)

            @pl.loop(0, per)
            def _(i):
                n = m * per + i

                @pl.when(jnp.logical_or(end == 0, j == nrow - 1))
                def _():
                    step(j, n + LAG)

                @pl.when(jnp.logical_and(j == 1, n < nblk // 2))
                def _():
                    invert(n * 2)
                    invert(n * 2 + 1)

                @pl.when(jnp.logical_and(j == 1, n == nblk // 2))
                def _():
                    publish()

                @pl.when(jnp.logical_and(j == nrow - 1, n < nportion))
                def _():
                    portion(n)

                @pl.when(jnp.logical_and(j == nrow - 1, n == nportion))
                def _():
                    write_early().start()

    @pl.loop(0, nblk)
    def _(g):
        wait_sent(g)

    for k in range(1, ncol):
        amps_copy(k).wait_send()

    @pl.loop(0, ncol)
    def _(cs):
        landed(nrow - 1, cs)

    write_early().wait()


def exchange(amps, integrals, mask, order, spots, nrow, ncol):
    arows, depth = amps.shape
    cols = integrals.shape[1]
    nblk = nrow * ncol
    rows = arows * ncol // nrow
    units = rows * cols // TILE
    cap = units // nblk
    nsl = cols // SLICE
    nk = (nrow - 1) * ncol
    any_spec = pl.BlockSpec(memory_space=pl.ANY)
    dma = pltpu.SemaphoreType.DMA
    got, gotp, pre, _, _, _ = pl.pallas_call(
        functools.partial(exchange_kernel, nrow, ncol),
        out_shape=[
            jax.ShapeDtypeStruct((nblk, cap, TILE), F32),
            jax.ShapeDtypeStruct((nblk, 1, cap), jnp.int32),
            jax.ShapeDtypeStruct((units, TILE), F32),
            jax.ShapeDtypeStruct((ncol, arows, depth), F32),
            jax.ShapeDtypeStruct((nrow * units,), jnp.int32),
            jax.ShapeDtypeStruct((nrow * nblk, 1, cap), jnp.int32),
        ],
        in_specs=[pl.BlockSpec(memory_space=pltpu.SMEM)] + [any_spec] * 4,
        out_specs=[any_spec] * 6,
        scratch_shapes=[
            pltpu.VMEM((2 * SLICE // TILE * depth, TILE), F32),
            pltpu.VMEM((2, arows // 2, depth), F32),
            pltpu.VMEM((rows, depth), BF16),
            pltpu.VMEM((rows, depth), BF16),
            pltpu.VMEM((nsl // 2, depth, SLICE), BF16),
            pltpu.VMEM((nsl // 2, depth, SLICE), BF16),
            pltpu.VMEM((nsl // 2, depth, SLICE), BF16),
            pltpu.VMEM((nsl // 2, depth, SLICE), BF16),
            pltpu.VMEM((units, TILE), F32),
            pltpu.VMEM((nblk, cap, TILE), F32),
            pltpu.VMEM((nk, cap, TILE), F32),
            pltpu.VMEM((nk, cap, TILE), F32),
            pltpu.SMEM((nrow * units,), jnp.int32),
            pltpu.VMEM((nblk, 1, cap), jnp.int32),
            pltpu.VMEM((2 * units // TILE, TILE), F32),
            pltpu.VMEM((units // TILE, TILE), jnp.int32),
            pltpu.SMEM((units // TILE, TILE), jnp.int32),
            dma((ncol,)), dma((ncol,)), dma((nrow,)), dma((nrow,)), dma((nrow,)), dma((nrow,)),
            dma((nblk,)), dma((nblk,)),
            dma((nk,)), dma((nk,)), dma((nk,)), dma((nk,)), dma((ncol,)), dma((nblk,)),
            dma((2 * SLICE // TILE,)), dma((8,)),
            pltpu.SemaphoreType.REGULAR, pltpu.SemaphoreType.REGULAR,
        ],
        compiler_params=pltpu.CompilerParams(
            collective_id=0, has_side_effects=True, vmem_limit_bytes=67043328),
        name="exchange",
    )(mask, amps, integrals, order, spots)
    return got, gotp, pre


def place_kernel(nrow, ncol, tpb, spot_ref, mask_ref, got, pre, den_ref, cyc_ref, upd_ref, term_ref,
                 moved, late, c_hi, c_lo, sems):
    rows = den_ref.shape[0]
    cap = got.shape[1]
    k = pl.program_id(0)

    @pl.when(k == 0)
    def _():
        copies = [pltpu.make_async_copy(pre, moved, sems.at[ncol])]
        slots = []
        for cs in range(ncol):
            j = nrow - 1
            n = ((cs // 4 + j // 2) % 2 * 2 + (cs // 2 % 2 + j % 2) % 2) * ncol + cs
            slots.append(n)
            copies.append(pltpu.make_async_copy(got.at[n], late.at[cs], sems.at[cs]))
        for copy in copies:
            copy.start()
        for copy in copies:
            copy.wait()
        for cs in range(ncol):
            @pl.loop(0, cap // UNROLL)
            def _(i):
                first = slots[cs] * cap + i * UNROLL
                for u in range(UNROLL):
                    moved[pl.ds(spot_ref[first + u], 1), :] = late[cs, pl.ds(i * UNROLL + u, 1), :]

    rb = tpb * TILE
    for w in range(PAIR):
        blk = k * PAIR + w
        for u in range(tpb):
            for s in range(tpb):
                at = (pl.ds(u * TILE, TILE), pl.ds(s * TILE, TILE))
                present = mask_ref[s, blk * tpb + u].astype(F32)
                hi, lo = split(cyc_ref[pl.ds(w * rb + u * TILE, TILE), pl.ds(s * TILE, TILE)] * present)
                c_hi[(w,) + at] = hi
                c_lo[(w,) + at] = lo
    for w in range(PAIR):
        blk = k * PAIR + w
        cols = pl.ds(w * rb, rb)
        tiles = [moved[pl.ds(pl.multiple_of((blk * tpb + t) * rows, rows), rows), :] for t in range(tpb)]
        upd = jnp.concatenate(tiles, axis=1) / den_ref[:, cols]
        upd_ref[:, cols] = upd
        hi, lo = split(upd)
        term_ref[:, cols] = dot(hi, c_hi[w]) + dot(lo, c_hi[w]) + dot(hi, c_lo[w])


def place(got, gotp, pre, nrow, ncol, denominators, cycle_tiles, cycle_mask):
    rows, cols = denominators.shape
    rb = cycle_tiles.shape[1]
    units = rows * cols // TILE
    out = jax.ShapeDtypeStruct((rows, cols), F32)
    block = pl.BlockSpec((rows, PAIR * rb), lambda i, s, m: (0, i))
    return pl.pallas_call(
        functools.partial(place_kernel, nrow, ncol, rb // TILE),
        out_shape=[out, out],
        grid_spec=pltpu.PrefetchScalarGridSpec(
            num_scalar_prefetch=2,
            grid=(cols // rb // PAIR,),
            in_specs=[
                pl.BlockSpec(memory_space=pl.ANY),
                pl.BlockSpec(memory_space=pl.ANY),
                block,
                pl.BlockSpec((PAIR * rb, rb), lambda i, s, m: (i, 0)),
            ],
            out_specs=[block, block],
            scratch_shapes=[
                pltpu.VMEM((units, TILE), F32),
                pltpu.VMEM((ncol,) + got.shape[1:], F32),
                pltpu.VMEM((PAIR, rb, rb), BF16),
                pltpu.VMEM((PAIR, rb, rb), BF16),
                pltpu.SemaphoreType.DMA((ncol + 1,)),
            ],
        ),
        compiler_params=pltpu.CompilerParams(vmem_limit_bytes=62 * 2**20),
        name="place",
    )(gotp.reshape(-1), cycle_mask.T, got, pre, denominators, cycle_tiles)


def sorted_keys(destination, nrow, ncol):
    rows, tiles = destination.shape
    vt = tiles * ncol
    units = rows * tiles
    flat = destination.T.reshape(-1)
    out_row = flat // vt
    out_tile = flat % vt
    owner = out_row // rows * ncol + out_tile // tiles
    spot = out_tile % tiles * rows + out_row % rows
    key = (owner * units + spot) * units + lax.iota(jnp.int32, units)
    ndev = nrow * ncol
    key = lax.sort(key, is_stable=False)
    return key % units, (key // units % units).reshape(ndev, 1, units // ndev)


def direct(amplitudes, integrals, integral_mask, denominators, cycle_tiles, cycle_mask, destination):
    nrow = lax.axis_size("row")
    ncol = lax.axis_size("col")
    order, spots = sorted_keys(destination, nrow, ncol)
    got, gotp, pre = exchange(amplitudes, integrals, integral_mask, order, spots, nrow, ncol)
    return tuple(place(got, gotp, pre, nrow, ncol, denominators, cycle_tiles, cycle_mask))


def solution(mesh):
    step = direct if (mesh.shape["row"], mesh.shape["col"]) == (4, 8) else body
    return jax.shard_map(
        step,
        mesh=mesh,
        in_specs=(
            P("col", "row"),
            P("row", "col"),
            P("row", "col"),
            P("row", "col"),
            P("col", None),
            P("col", None),
            P("row", "col"),
        ),
        out_specs=(P("row", "col"), P("row", "col")),
        check_vma=False,
    )
```

```python
import functools
import jax
import jax.numpy as jnp
from jax import lax
from jax.experimental import pallas as pl
from jax.experimental.pallas import tpu as pltpu
from jax.sharding import PartitionSpec as P

TILE = 128
F32 = jnp.float32
BF16 = jnp.bfloat16
CHUNKS = 4


def split(x):
    hi = x.astype(BF16)
    return hi, (x - hi.astype(F32)).astype(BF16)


def dot(a, b):
    return jnp.dot(a, b, preferred_element_type=F32)


def product_kernel(nblk, first_tile, tpb, off_ref, mask_ref, a_ref, b_ref, *rest):
    outs, (a_hi, a_lo, b_hi, b_lo) = rest[:-4], rest[-4:]
    rows, depth = a_ref.shape
    blk = rows // nblk
    step = pl.program_id(0)

    @pl.when(step == 0)
    def _():
        for j in range(nblk):
            src = pl.multiple_of(off_ref[j] * blk, blk)
            hi, lo = split(a_ref[pl.ds(src, blk), :])
            a_hi[pl.ds(j * blk, blk), :] = hi
            a_lo[pl.ds(j * blk, blk), :] = lo

    @pl.loop(0, depth // TILE)
    def _(c):
        at = pl.ds(pl.multiple_of(c * TILE, TILE), TILE)
        for t in range(tpb):
            cols = pl.ds(t * TILE, TILE)
            m = mask_ref[c, first_tile + step * tpb + t].astype(F32)
            hi, lo = split(b_ref[at, cols] * m)
            b_hi[at, cols] = hi
            b_lo[at, cols] = lo

    big = rows // 2
    piece = rows // len(outs)
    per = big // piece if big >= piece else 1
    for h in range(2):
        at = pl.ds(h * big, big)
        acc = dot(a_hi[at, :], b_hi[...]) + dot(a_lo[at, :], b_hi[...]) + dot(a_hi[at, :], b_lo[...])
        for t in range(tpb):
            col = acc[:, t * TILE:(t + 1) * TILE]
            if len(outs) == 1:
                outs[0][t, at, :] = col
            else:
                for q in range(per):
                    outs[h * per + q][t, :, :] = col[q * piece:(q + 1) * piece]


def product(amps, integrals, mask, offsets, chunk, nblk, npieces):
    rows, depth = amps.shape
    cols = integrals.shape[1]
    width = cols // CHUNKS
    tpb = min(4, width // TILE)
    bn = tpb * TILE
    steps = width // bn
    piece = rows // npieces
    out = jax.ShapeDtypeStruct((width // TILE, piece, TILE), F32)
    return pl.pallas_call(
        functools.partial(product_kernel, nblk, chunk * (width // TILE), tpb),
        out_shape=[out] * npieces,
        grid_spec=pltpu.PrefetchScalarGridSpec(
            num_scalar_prefetch=2,
            grid=(steps,),
            in_specs=[
                pl.BlockSpec((rows, depth), lambda i, o, m: (0, 0), pipeline_mode=pl.Buffered(1)),
                pl.BlockSpec((depth, bn), lambda i, o, m: (0, chunk * steps + i)),
            ],
            out_specs=[pl.BlockSpec((tpb, piece, TILE), lambda i, o, m: (i, 0, 0))] * npieces,
            scratch_shapes=[
                pltpu.VMEM((rows, depth), BF16),
                pltpu.VMEM((rows, depth), BF16),
                pltpu.VMEM((depth, bn), BF16),
                pltpu.VMEM((depth, bn), BF16),
            ],
        ),
        cost_estimate=pl.CostEstimate(
            flops=6 * rows * depth * width,
            bytes_accessed=4 * (rows * depth + depth * width + rows * width),
            transcendentals=0,
        ),
        compiler_params=pltpu.CompilerParams(vmem_limit_bytes=56 * 2**20),
        name="product",
    )(offsets, mask, amps, integrals)


def gather_kernel(idx_ref, x_ref, o_ref):
    n = o_ref.shape[0]
    base = pl.program_id(0) * n

    @pl.loop(0, n // 16)
    def _(i):
        for u in range(16):
            k = i * 16 + u
            o_ref[pl.ds(k, 1), :] = x_ref[pl.ds(idx_ref[base + k], 1), :]


def gather_units(units, idx):
    n = units.shape[0]
    bn = min(1024, n)
    return pl.pallas_call(
        gather_kernel,
        out_shape=jax.ShapeDtypeStruct(units.shape, F32),
        grid_spec=pltpu.PrefetchScalarGridSpec(
            num_scalar_prefetch=1,
            grid=(n // bn,),
            in_specs=[pl.BlockSpec(units.shape, lambda i, s: (0, 0), pipeline_mode=pl.Buffered(1))],
            out_specs=pl.BlockSpec((bn, TILE), lambda i, s: (i, 0)),
        ),
        compiler_params=pltpu.CompilerParams(vmem_limit_bytes=24 * 2**20),
        name="gather_units",
    )(idx, units)


def finish_kernel(tiles, tpb, idx_ref, mask_ref, got_ref, den_ref, cyc_ref, upd_ref, term_ref, moved, c_hi, c_lo):
    rows = den_ref.shape[0]
    k = pl.program_id(0)

    @pl.loop(0, rows // 8)
    def _(i):
        for u in range(8):
            r = i * 8 + u
            for t in range(tpb):
                q = idx_ref[r * tiles + k * tpb + t]
                moved[t, pl.ds(r, 1), :] = got_ref[pl.ds(q, 1), :]

    for u in range(tpb):
        for s in range(tpb):
            at = (pl.ds(u * TILE, TILE), pl.ds(s * TILE, TILE))
            hi, lo = split(cyc_ref[at] * mask_ref[k * tpb + u, s].astype(F32))
            c_hi[at] = hi
            c_lo[at] = lo
    upd = jnp.concatenate([moved[t] for t in range(tpb)], axis=1) / den_ref[...]
    upd_ref[...] = upd
    hi, lo = split(upd)
    term_ref[...] = dot(hi, c_hi[...]) + dot(lo, c_hi[...]) + dot(hi, c_lo[...])


def finish(got, inv, denominators, cycle_tiles, cycle_mask):
    rows, cols = denominators.shape
    rb = cycle_tiles.shape[1]
    out = jax.ShapeDtypeStruct((rows, cols), F32)
    block = pl.BlockSpec((rows, rb), lambda i, s, m: (0, i))
    return pl.pallas_call(
        functools.partial(finish_kernel, cols // TILE, rb // TILE),
        out_shape=[out, out],
        grid_spec=pltpu.PrefetchScalarGridSpec(
            num_scalar_prefetch=2,
            grid=(cols // rb,),
            in_specs=[
                pl.BlockSpec(got.shape, lambda i, s, m: (0, 0), pipeline_mode=pl.Buffered(1)),
                block,
                pl.BlockSpec((rb, rb), lambda i, s, m: (i, 0)),
            ],
            out_specs=[block, block],
            scratch_shapes=[
                pltpu.VMEM((rb // TILE, rows, TILE), F32),
                pltpu.VMEM((rb, rb), BF16),
                pltpu.VMEM((rb, rb), BF16),
            ],
        ),
        compiler_params=pltpu.CompilerParams(vmem_limit_bytes=40 * 2**20),
        name="finish",
    )(inv, cycle_mask, got, denominators, cycle_tiles)


def routes(destination, nrow, ncol):
    local_rows, local_tiles = destination.shape
    vt = local_tiles * ncol
    units = local_rows * local_tiles
    half = local_rows // 2
    tc = local_tiles // CHUNKS
    flat = destination.reshape(2, half, CHUNKS, tc).transpose(2, 0, 3, 1).reshape(-1)
    out_row = flat // vt
    out_tile = flat % vt
    owner = out_row // local_rows * ncol + out_tile // local_tiles
    place = out_row % local_rows * local_tiles + out_tile % local_tiles
    iota = lax.iota(jnp.int32, units)
    key, order = lax.sort((owner * units + place, iota), num_keys=1, is_stable=False)
    ndev = nrow * ncol
    places = (key % units).astype(F32).reshape(ndev, units // ndev)
    got_place = lax.all_to_all(places, ("row", "col"), split_axis=0, concat_axis=0, tiled=True)
    _, inv = lax.sort((got_place.reshape(-1).astype(jnp.int32), iota), num_keys=1, is_stable=False)
    return order, inv


def body(amplitudes, integrals, integral_mask, denominators, cycle_tiles, cycle_mask, destination):
    nrow = lax.axis_size("row")
    ncol = lax.axis_size("col")
    me = lax.axis_index("row")
    amps = lax.all_gather(amplitudes, "col", axis=0, tiled=True)
    order, inv = routes(destination, nrow, ncol)
    local_rows = destination.shape[0]
    half = local_rows // 2
    pieces = []
    if nrow == 4:
        up = [(i, (i + 1) % nrow) for i in range(nrow)]
        down = [(i, (i - 1) % nrow) for i in range(nrow)]
        offsets = jnp.stack([(me + d) % nrow for d in (2, 1, 3, 0)]).astype(jnp.int32)
        sent, landed = [], []
        for c in range(CHUNKS):
            if c >= 2:
                after = sent[c - 2] + (landed[c - 3] if c >= 3 else [])
                offsets = lax.optimization_barrier([offsets] + after)[0]
            far_a, far_b, up_a, up_b, dn_a, dn_b, own_a, own_b = product(
                amps, integrals, integral_mask, offsets, c, nrow, 2 * nrow)
            in_a = lax.ppermute(far_a, "row", up)
            in_b = lax.ppermute(far_b, "row", down)
            direct_b = lax.ppermute(up_b, "row", up)
            direct_a = lax.ppermute(dn_a, "row", down)
            next_a, next_b = up_a + in_a, dn_b + in_b
            sum_a = lax.ppermute(next_a, "row", up)
            sum_b = lax.ppermute(next_b, "row", down)
            sent.append([next_a, next_b, direct_a, direct_b])
            landed.append([sum_a, sum_b])
            pieces.append(own_a + direct_a + sum_a)
            pieces.append(own_b + direct_b + sum_b)
    else:
        offsets = lax.iota(jnp.int32, nrow)
        for c in range(CHUNKS):
            (part,) = product(amps, integrals, integral_mask, offsets, c, nrow, 1)
            summed = lax.psum_scatter(part, "row", scatter_dimension=1, tiled=True)
            pieces.append(summed[:, :half])
            pieces.append(summed[:, half:])
    units = jnp.concatenate([p.reshape(-1, TILE) for p in pieces], axis=0)
    sending = gather_units(units, order)
    ndev = nrow * ncol
    got = lax.all_to_all(sending.reshape(ndev, -1, TILE), ("row", "col"), split_axis=0, concat_axis=0, tiled=True)
    return tuple(finish(got.reshape(-1, TILE), inv, denominators, cycle_tiles, cycle_mask))


MESH = pl.DeviceIdType.MESH
SLICE = 512
UNROLL = 16
LAG = 4
PORTION = 4
PAIR = 2


def exchange_kernel(nrow, ncol, mask_ref, amps, integ, order, spots, got, gotp, pre, aall, oall, pall,
                    st, ast, ah, al, bh0, bl0, bh1, bl1, part, group, ru, rd, idx, spot, total, found, inv,
                    a_s, a_r, o_s, o_r, q_s, q_r, p_s, p_r, u_s, u_r, d_s, d_r, f_s, f_r, b_sem, l_sem, credit_u, credit_d):
    z = lax.axis_index("row")
    c = lax.axis_index("col")
    last = nrow - 1
    arows, depth = amps.shape
    nblk, cap = got.shape[0], got.shape[1]
    units = nblk * cap
    half, _, width = bh0.shape
    nsl = half * 2
    bands = (bh0, bl0), (bh1, bl1)
    tps = width // TILE
    rows = ah.shape[0]
    nk = last * ncol
    low = 1 - z // 2
    inner = z * (last - z)
    end = 1 - (inner + 1) // 2
    core = c % 2
    cx = c // 2 % 2
    cy = c // 4

    def peer(k):
        px = (cx + k // 2 % 2) % 2
        py = (cy + k // 4) % 2
        return (py * 2 + px) * 2 + (core + k % 2) % 2

    def col_of(i):
        return peer(ncol - 1 - i)

    def block_of(j):
        return (cy + j // 2) % 2 * 2 + (cx + j % 2) % 2

    def amps_copy(k):
        return pltpu.make_async_remote_copy(amps, aall.at[c], a_s.at[k], a_r.at[k], (z, peer(k)), MESH)

    def order_copy(dz):
        at = pl.ds(pl.multiple_of(z * units, units), units)
        return pltpu.make_async_remote_copy(order, oall.at[at], o_s.at[dz], o_r.at[dz], ((z + dz) % nrow, c), MESH)

    def spots_copy(dz):
        return pltpu.make_async_remote_copy(
            spots, pall.at[pl.ds(z * nblk, nblk)], q_s.at[dz], q_r.at[dz], ((z + dz) % nrow, c), MESH)

    def up_copy(k):
        g = (last - k // ncol) * ncol + k % ncol
        return pltpu.make_async_remote_copy(group.at[g], ru.at[k], u_s.at[k], u_r.at[k], ((z + 1) % nrow, c), MESH)

    def down_copy(k):
        return pltpu.make_async_remote_copy(
            group.at[k], rd.at[k], d_s.at[k], d_r.at[k], ((z + nrow - 1) % nrow, c), MESH)

    def final_copy(j, i):
        s = block_of(j) * ncol + c
        return pltpu.make_async_remote_copy(
            group.at[z * ncol + i], got.at[s], f_s.at[i], f_r.at[s], (z, col_of(i)), MESH)

    def final_local(j):
        own = ncol - 1
        return pltpu.make_async_copy(group.at[z * ncol + own], got.at[block_of(j) * ncol + c], f_s.at[own])

    def load_cols(s, slot):
        return [pltpu.make_async_copy(
            integ.at[:, pl.ds(pl.multiple_of((s * tps + t) * TILE, TILE), TILE)],
            st.at[pl.ds((slot * tps + t) * depth, depth)], b_sem.at[slot * tps + t]) for t in range(tps)]

    def fetch(s, slot):
        for copy in load_cols(s, slot):
            copy.start()

    def arrive(s, slot):
        for copy in load_cols(s, slot):
            copy.wait()

    def load_amps(j):
        r = block_of(j)
        part_rows = arows // 2

        def begin(q):
            e, h = q // 2, q % 2
            i = (e + core) % 2
            at = pl.ds(h * part_rows, part_rows)
            own = (j + e) == 0

            @pl.when(own)
            def _():
                pltpu.make_async_copy(amps.at[at], ast.at[h], l_sem.at[h]).start()

            @pl.when(jnp.logical_not(own))
            def _():
                if h == 0:
                    amps_copy(j * 2 + e).wait_recv()
                pltpu.make_async_copy(aall.at[r * 2 + i, at], ast.at[h], l_sem.at[h]).start()

        begin(0)
        begin(1)
        for q in range(4):
            h = q % 2
            pltpu.make_async_copy(amps.at[pl.ds(0, part_rows)], ast.at[h], l_sem.at[h]).wait()

            @pl.loop(0, part_rows // 16)
            def _(n):
                at = pl.ds(pl.multiple_of(n * 16, 16), 16)
                half_at = (q // 2 + core) % 2 * 2 + q % 2
                to = pl.ds(pl.multiple_of(half_at * part_rows + n * 16, 16), 16)
                hi, lo = split(ast[h, at, :])
                ah[to, :] = hi
                al[to, :] = lo

            if q < 2:
                begin(q + 2)

    def dots(m, odd):
        bh, bl = bands[odd]
        acc = dot(ah[...], bh[m]) + dot(al[...], bh[m]) + dot(ah[...], bl[m])
        for t in range(tps):
            at = pl.ds(pl.multiple_of(((m * 2 + odd) * tps + t) * rows, rows), rows)
            part[at, :] = acc[:, t * TILE:(t + 1) * TILE]

    def split_cols(m, odd):
        bh, bl = bands[odd]
        for n in range(depth // TILE):
            at = pl.ds(n * TILE, TILE)
            for t in range(tps):
                cols = pl.ds(t * TILE, TILE)
                rows_at = pl.ds((odd * tps + t) * depth + n * TILE, TILE)
                hi, lo = split(st[rows_at, :] * mask_ref[n, (m * 2 + odd) * tps + t].astype(F32))
                bh[m, at, cols] = hi
                bl[m, at, cols] = lo

    for slot in range(2):
        fetch(slot, slot)
    barrier = pltpu.get_barrier_semaphore()
    for k in range(1, ncol):
        pl.semaphore_signal(barrier, 1, device_id=(z, peer(k)), device_id_type=MESH)
    for dz in range(1, nrow):
        pl.semaphore_signal(barrier, 1, device_id=((z + dz) % nrow, c), device_id_type=MESH)
    pl.semaphore_wait(barrier, ncol - 1 + nrow - 1)

    for dz in range(1, nrow):
        order_copy(dz).start()
        spots_copy(dz).start()
    for k in range(1, ncol):
        amps_copy(k).start()
    def to_scalar(src, r, n):
        at = pl.ds(pl.multiple_of(r * units, units), units)
        return pltpu.make_async_copy(src, idx.at[at], l_sem.at[2 + n])

    own_order = to_scalar(order, z, 0)
    own_order.start()

    arrive(0, 0)
    split_cols(0, 0)
    fetch(2, 0)
    load_amps(0)
    own_order.wait()
    for dz in range(1, nrow):
        order_copy(dz).wait()
        r = (z + nrow - dz) % nrow
        to_scalar(oall.at[pl.ds(pl.multiple_of(r * units, units), units)], r, dz).start()

    @pl.loop(0, half - 1)
    def _(m):
        arrive(m * 2 + 1, 1)
        split_cols(m, 1)
        dots(m, 0)
        fetch(m * 2 + 3, 1)
        arrive(m * 2 + 2, 0)
        split_cols(m + 1, 0)
        dots(m, 1)

        @pl.when(m < half - 2)
        def _():
            fetch(m * 2 + 4, 0)

    arrive(nsl - 1, 1)
    split_cols(half - 1, 1)
    dots(half - 1, 0)
    dots(half - 1, 1)
    for dz in range(1, nrow):
        to_scalar(order, 0, dz).wait()

    def places_remote(src, r, cc):
        return pltpu.make_async_remote_copy(
            src, gotp.at[r * ncol + c], p_s.at[r * ncol + cc], p_r.at[r * ncol + c], (z, cc), MESH)

    def places_local(src, r):
        return pltpu.make_async_copy(src, gotp.at[r * ncol + c], p_s.at[r * ncol + c])

    def send_places(n):
        r = n // ncol
        cc = n % ncol
        g = z * ncol + cc

        @pl.when(jnp.logical_and(cc == c, r == z))
        def _():
            places_local(spots.at[g], r).start()

        @pl.when(jnp.logical_and(cc == c, r != z))
        def _():
            places_local(pall.at[r * nblk + g], r).start()

        @pl.when(jnp.logical_and(cc != c, r == z))
        def _():
            places_remote(spots.at[g], r, cc).start()

        @pl.when(jnp.logical_and(cc != c, r != z))
        def _():
            places_remote(pall.at[r * nblk + g], r, cc).start()

    def wait_places():
        @pl.loop(0, nblk)
        def _(n):
            cc = n % ncol

            @pl.when(cc == c)
            def _():
                places_local(spots.at[0], n // ncol).wait()

            @pl.when(cc != c)
            def _():
                places_remote(spots.at[0], n // ncol, cc).wait_send()
                pltpu.make_async_copy(spots.at[0], gotp.at[n], p_r.at[n]).wait()

    lines = units // TILE

    def invert(n):
        lane = lax.broadcasted_iota(jnp.int32, (1, cap), 1)
        at = spot[n]
        high = jnp.right_shift(at, TILE.bit_length() - 1)
        here = lax.broadcasted_iota(jnp.int32, (lines, cap), 0) == high
        slot_high = (n * (cap // TILE) + lane // TILE).astype(F32)
        slot_low = (lane % TILE).astype(F32)
        left = jnp.concatenate(
            [jnp.where(here, slot_high, 0.0), jnp.where(here, slot_low, 0.0)], axis=0).astype(BF16)
        low_here = lax.broadcasted_iota(jnp.int32, (TILE, cap), 0) == jnp.bitwise_and(at, TILE - 1)
        right = jnp.where(low_here, 1.0, 0.0).astype(BF16)
        total[...] += lax.dot_general(left, right, (((1,), (1,)), ((), ())), preferred_element_type=F32)

    def publish():
        slot = (total[:lines, :] * TILE + total[lines:, :]).astype(jnp.int32)
        found[...] = jnp.clip(slot, 0, units - 1)
        copy = pltpu.make_async_copy(found, inv, l_sem.at[6])
        copy.start()
        copy.wait()

    def source_slot(j, cs):
        return ((cs // 4 + j // 2) % 2 * 2 + (cs // 2 % 2 + j % 2) % 2) * ncol + cs

    def landed(j, cs):
        n = source_slot(j, cs)

        @pl.when(cs != c)
        def _():
            pltpu.make_async_copy(group.at[0], got.at[n], f_r.at[n]).wait()

        return n

    early = nk * cap

    def gather_early():
        @pl.loop(0, nk)
        def _(t):
            n = landed(t // ncol, t % ncol)
            pltpu.make_async_copy(got.at[n], st.at[pl.ds(pl.multiple_of(n * cap, cap), cap)], l_sem.at[6]).start()

        pltpu.make_async_copy(pre.at[pl.ds(0, early)], st.at[pl.ds(0, early)], l_sem.at[6]).wait()

    def portion(k):
        @pl.loop(0, PORTION)
        def _(a):
            line = k * PORTION + a
            for u in range(TILE):
                part[pl.ds(line * TILE + u, 1), :] = st[pl.ds(inv[line, u], 1), :]

    def write_early():
        return pltpu.make_async_copy(part, pre, l_sem.at[7])

    def step(j, k):
        more = j < nrow - 1
        ku = k - (1 - low) * LAG
        kd = k - low * LAG
        d = last - ku // ncol

        @pl.when(jnp.logical_and(jnp.logical_and(z >= 1, ku >= 0), d >= z))
        def _():
            up_copy(ku).wait_recv()
            group[d * ncol + ku % ncol] += ru[ku]

            @pl.when(more)
            def _():
                pl.semaphore_signal(credit_u, 1, device_id=((z + nrow - 1) % nrow, c), device_id_type=MESH)

            @pl.when(d > z)
            def _():
                @pl.when(j > 0)
                def _():
                    pl.semaphore_wait(credit_u, 1)

                up_copy(ku).start()

        e = kd // ncol

        @pl.when(jnp.logical_and(jnp.logical_and(z < last, kd >= 0), e <= z))
        def _():
            down_copy(kd).wait_recv()
            group[kd] += rd[kd]

            @pl.when(more)
            def _():
                pl.semaphore_signal(credit_d, 1, device_id=((z + 1) % nrow, c), device_id_type=MESH)

            @pl.when(e < z)
            def _():
                @pl.when(j > 0)
                def _():
                    pl.semaphore_wait(credit_d, 1)

                down_copy(kd).start()

        kf = k - end * LAG + ncol
        i = kf % ncol

        @pl.when(kf // ncol == inner + 1)
        def _():
            @pl.when(i == ncol - 1)
            def _():
                final_local(j).start()

            @pl.when(i < ncol - 1)
            def _():
                final_copy(j, i).start()

    def wait_sent(g):
        d = g // ncol
        i = g % ncol

        @pl.when(d > z)
        def _():
            up_copy((last - d) * ncol + i).wait_send()

        @pl.when(d < z)
        def _():
            down_copy(g).wait_send()

        @pl.when(jnp.logical_and(d == z, i == ncol - 1))
        def _():
            final_local(0).wait()

        @pl.when(jnp.logical_and(d == z, i < ncol - 1))
        def _():
            final_copy(0, i).wait_send()

    gap = nk // LAG
    per = (nk - LAG) // half
    nportion = units // TILE // PORTION

    @pl.loop(0, nrow)
    def _(j):
        base = block_of(j) * units

        def order_piece(n):
            q = n // ncol
            p = n % ncol
            d = low * (last - q) + (1 - low) * q
            g = d * ncol + p
            start = base + (d * ncol + col_of(p)) * cap

            @pl.when(j > 0)
            def _():
                wait_sent(g)

            @pl.loop(0, cap // UNROLL)
            def _(i):
                first = start + i * UNROLL
                for u in range(UNROLL):
                    group[g, pl.ds(i * UNROLL + u, 1), :] = part[pl.ds(idx[first + u], 1), :]

            @pl.when(jnp.logical_and(z == 0, d > 0))
            def _():
                @pl.when(j > 0)
                def _():
                    pl.semaphore_wait(credit_u, 1)

                up_copy((last - d) * ncol + p).start()

            @pl.when(jnp.logical_and(z == last, d < last))
            def _():
                @pl.when(j > 0)
                def _():
                    pl.semaphore_wait(credit_d, 1)

                down_copy(g).start()

            @pl.when(jnp.logical_and(jnp.logical_and(end == 0, n < LAG * gap), n % gap == gap - 1))
            def _():
                step(j, n // gap)

        pl.loop(0, nk)(order_piece)

        @pl.when(jnp.logical_and(j > 0, end == 1))
        def _():
            @pl.loop(0, nk)
            def _(k):
                step(j - 1, k)

        pl.loop(nk, nblk)(order_piece)

        @pl.when(j == 0)
        def _():
            for dz in range(1, nrow):
                spots_copy(dz).wait()
            pl.loop(0, nblk)(send_places)

        @pl.when(j == 1)
        def _():
            wait_places()
            copy = pltpu.make_async_copy(gotp, spot, l_sem.at[6])
            copy.start()
            copy.wait()
            total[...] = jnp.zeros_like(total)

        @pl.when(j < nrow - 1)
        def _():
            load_amps(j + 1)

        @pl.when(j == nrow - 1)
        def _():
            gather_early()

        @pl.loop(0, half)
        def _(m):
            @pl.when(j < nrow - 1)
            def _():
                dots(m, 0)
                dots(m, 1)

            @pl.loop(0, per)
            def _(i):
                n = m * per + i

                @pl.when(jnp.logical_or(end == 0, j == nrow - 1))
                def _():
                    step(j, n + LAG)

                @pl.when(jnp.logical_and(j == 1, n < nblk // 2))
                def _():
                    invert(n * 2)
                    invert(n * 2 + 1)

                @pl.when(jnp.logical_and(j == 1, n == nblk // 2))
                def _():
                    publish()

                @pl.when(jnp.logical_and(j == nrow - 1, n < nportion))
                def _():
                    portion(n)

                @pl.when(jnp.logical_and(j == nrow - 1, n == nportion))
                def _():
                    write_early().start()

    @pl.loop(0, nblk)
    def _(g):
        wait_sent(g)

    for k in range(1, ncol):
        amps_copy(k).wait_send()

    @pl.loop(0, ncol)
    def _(cs):
        landed(nrow - 1, cs)

    write_early().wait()


def exchange(amps, integrals, mask, order, spots, nrow, ncol):
    arows, depth = amps.shape
    cols = integrals.shape[1]
    nblk = nrow * ncol
    rows = arows * ncol // nrow
    units = rows * cols // TILE
    cap = units // nblk
    nsl = cols // SLICE
    nk = (nrow - 1) * ncol
    any_spec = pl.BlockSpec(memory_space=pl.ANY)
    dma = pltpu.SemaphoreType.DMA
    got, gotp, pre, _, _, _ = pl.pallas_call(
        functools.partial(exchange_kernel, nrow, ncol),
        out_shape=[
            jax.ShapeDtypeStruct((nblk, cap, TILE), F32),
            jax.ShapeDtypeStruct((nblk, 1, cap), jnp.int32),
            jax.ShapeDtypeStruct((units, TILE), F32),
            jax.ShapeDtypeStruct((ncol, arows, depth), F32),
            jax.ShapeDtypeStruct((nrow * units,), jnp.int32),
            jax.ShapeDtypeStruct((nrow * nblk, 1, cap), jnp.int32),
        ],
        in_specs=[pl.BlockSpec(memory_space=pltpu.SMEM)] + [any_spec] * 4,
        out_specs=[any_spec] * 6,
        scratch_shapes=[
            pltpu.VMEM((2 * SLICE // TILE * depth, TILE), F32),
            pltpu.VMEM((2, arows // 2, depth), F32),
            pltpu.VMEM((rows, depth), BF16),
            pltpu.VMEM((rows, depth), BF16),
            pltpu.VMEM((nsl // 2, depth, SLICE), BF16),
            pltpu.VMEM((nsl // 2, depth, SLICE), BF16),
            pltpu.VMEM((nsl // 2, depth, SLICE), BF16),
            pltpu.VMEM((nsl // 2, depth, SLICE), BF16),
            pltpu.VMEM((units, TILE), F32),
            pltpu.VMEM((nblk, cap, TILE), F32),
            pltpu.VMEM((nk, cap, TILE), F32),
            pltpu.VMEM((nk, cap, TILE), F32),
            pltpu.SMEM((nrow * units,), jnp.int32),
            pltpu.VMEM((nblk, 1, cap), jnp.int32),
            pltpu.VMEM((2 * units // TILE, TILE), F32),
            pltpu.VMEM((units // TILE, TILE), jnp.int32),
            pltpu.SMEM((units // TILE, TILE), jnp.int32),
            dma((ncol,)), dma((ncol,)), dma((nrow,)), dma((nrow,)), dma((nrow,)), dma((nrow,)),
            dma((nblk,)), dma((nblk,)),
            dma((nk,)), dma((nk,)), dma((nk,)), dma((nk,)), dma((ncol,)), dma((nblk,)),
            dma((2 * SLICE // TILE,)), dma((8,)),
            pltpu.SemaphoreType.REGULAR, pltpu.SemaphoreType.REGULAR,
        ],
        compiler_params=pltpu.CompilerParams(
            collective_id=0, has_side_effects=True, vmem_limit_bytes=67043328),
        name="exchange",
    )(mask, amps, integrals, order, spots)
    return got, gotp, pre


def place_kernel(nrow, ncol, tpb, spot_ref, mask_ref, got, pre, den_ref, cyc_ref, upd_ref, term_ref,
                 moved, late, c_hi, c_lo, sems):
    rows = den_ref.shape[0]
    cap = got.shape[1]
    k = pl.program_id(0)

    @pl.when(k == 0)
    def _():
        copies = [pltpu.make_async_copy(pre, moved, sems.at[ncol])]
        slots = []
        for cs in range(ncol):
            j = nrow - 1
            n = ((cs // 4 + j // 2) % 2 * 2 + (cs // 2 % 2 + j % 2) % 2) * ncol + cs
            slots.append(n)
            copies.append(pltpu.make_async_copy(got.at[n], late.at[cs], sems.at[cs]))
        for copy in copies:
            copy.start()
        for copy in copies:
            copy.wait()
        for cs in range(ncol):
            @pl.loop(0, cap // UNROLL)
            def _(i):
                first = slots[cs] * cap + i * UNROLL
                for u in range(UNROLL):
                    moved[pl.ds(spot_ref[first + u], 1), :] = late[cs, pl.ds(i * UNROLL + u, 1), :]

    rb = tpb * TILE
    for w in range(PAIR):
        blk = k * PAIR + w
        for u in range(tpb):
            for s in range(tpb):
                at = (pl.ds(u * TILE, TILE), pl.ds(s * TILE, TILE))
                present = mask_ref[s, blk * tpb + u].astype(F32)
                hi, lo = split(cyc_ref[pl.ds(w * rb + u * TILE, TILE), pl.ds(s * TILE, TILE)] * present)
                c_hi[(w,) + at] = hi
                c_lo[(w,) + at] = lo
    for w in range(PAIR):
        blk = k * PAIR + w
        cols = pl.ds(w * rb, rb)
        tiles = [moved[pl.ds(pl.multiple_of((blk * tpb + t) * rows, rows), rows), :] for t in range(tpb)]
        upd = jnp.concatenate(tiles, axis=1) / den_ref[:, cols]
        upd_ref[:, cols] = upd
        hi, lo = split(upd)
        term_ref[:, cols] = dot(hi, c_hi[w]) + dot(lo, c_hi[w]) + dot(hi, c_lo[w])


def place(got, gotp, pre, nrow, ncol, denominators, cycle_tiles, cycle_mask):
    rows, cols = denominators.shape
    rb = cycle_tiles.shape[1]
    units = rows * cols // TILE
    out = jax.ShapeDtypeStruct((rows, cols), F32)
    block = pl.BlockSpec((rows, PAIR * rb), lambda i, s, m: (0, i))
    return pl.pallas_call(
        functools.partial(place_kernel, nrow, ncol, rb // TILE),
        out_shape=[out, out],
        grid_spec=pltpu.PrefetchScalarGridSpec(
            num_scalar_prefetch=2,
            grid=(cols // rb // PAIR,),
            in_specs=[
                pl.BlockSpec(memory_space=pl.ANY),
                pl.BlockSpec(memory_space=pl.ANY),
                block,
                pl.BlockSpec((PAIR * rb, rb), lambda i, s, m: (i, 0)),
            ],
            out_specs=[block, block],
            scratch_shapes=[
                pltpu.VMEM((units, TILE), F32),
                pltpu.VMEM((ncol,) + got.shape[1:], F32),
                pltpu.VMEM((PAIR, rb, rb), BF16),
                pltpu.VMEM((PAIR, rb, rb), BF16),
                pltpu.SemaphoreType.DMA((ncol + 1,)),
            ],
        ),
        compiler_params=pltpu.CompilerParams(vmem_limit_bytes=62 * 2**20),
        name="place",
    )(gotp.reshape(-1), cycle_mask.T, got, pre, denominators, cycle_tiles)


def sorted_keys(destination, nrow, ncol):
    rows, tiles = destination.shape
    vt = tiles * ncol
    units = rows * tiles
    flat = destination.T.reshape(-1)
    out_row = flat // vt
    out_tile = flat % vt
    owner = out_row // rows * ncol + out_tile // tiles
    spot = out_tile % tiles * rows + out_row % rows
    key = (owner * units + spot) * units + lax.iota(jnp.int32, units)
    ndev = nrow * ncol
    key = lax.sort(key, is_stable=False)
    return key % units, (key // units % units).reshape(ndev, 1, units // ndev)


def direct(amplitudes, integrals, integral_mask, denominators, cycle_tiles, cycle_mask, destination):
    nrow = lax.axis_size("row")
    ncol = lax.axis_size("col")
    order, spots = sorted_keys(destination, nrow, ncol)
    got, gotp, pre = exchange(amplitudes, integrals, integral_mask, order, spots, nrow, ncol)
    return tuple(place(got, gotp, pre, nrow, ncol, denominators, cycle_tiles, cycle_mask))


def solution(mesh):
    step = direct if (mesh.shape["row"], mesh.shape["col"]) == (4, 8) else body
    return jax.shard_map(
        step,
        mesh=mesh,
        in_specs=(
            P("col", "row"),
            P("row", "col"),
            P("row", "col"),
            P("row", "col"),
            P("col", None),
            P("col", None),
            P("row", "col"),
        ),
        out_specs=(P("row", "col"), P("row", "col")),
        check_vma=False,
    )
```
